32 devices in a mesh: grp: 2 (over y), pulse: 16 (over z, x, core), rng: 1.
Axes of the slice: x: 2, y: 2, z: 4, core: 2. Of those that a mesh axis runs over, the one named last changes fastest.
Arguments:
- raw_echoes: bfloat16 [256, 64, 2, 128], P(('grp', 'pulse'), 'rng'), parts along dimension 0, may hold values from -6 to 6
- matched: float32 [2, 128], replicated, may hold values from -0.375 to 0.375
- delays: int32 [256, 16], P(('grp', 'pulse')), parts along dimension 0, may hold values from -24 to 24
- pulse_phase: float32 [256, 16], P(('grp', 'pulse')), parts along dimension 0, may hold values from -3.140625 to 3.140625
- beam_map: int32 [4, 2, 2, 16], replicated, may hold values from 0 to 15, as said below
- range_shift: int32 [4, 2, 2, 16], replicated, may hold values from -24 to 24
- phase_base: float32 [4, 2, 2, 16], replicated, may hold values from -3.140625 to 3.140625
- phase_rate: float32 [4, 2, 2, 16], replicated, may hold values from -4 to 4
- tap_offsets: int32 [4, 4], replicated, may hold values from -4 to 4, as said below
Outputs:
- final_image: float32 [2, 512, 8192], P(None, ('grp', 'pulse'), 'rng'), parts along dimension 1
The draws below stay inside these ranges and needn't reach their ends.
There are 2 independent parts, one for each index of `grp`. The reference program is written for one: setup_inputs(seed, part) draws one part's arguments, and reference() takes and returns one part's arrays. A program takes and returns all parts, laid end to end along the dimension named above; an argument that names none is the same for every part. Nothing has to cross between parts.
Inputs may be any that keep to these rules, and one draw needn't show every extreme that they name: `beam_map`: entry [l, h, s, k] is h * 8 + k // 2 plus -1, 0 or 1, clamped to the range. `tap_offsets`: the 4 entries of one level are distinct.
All inputs are finite; a program needn't handle non-finite values.
Results may differ from the reference program's by a relative error of at most 0.0055.
Values may be sent and summed in bfloat16 or wider, within the bound.
A program may use at most 64 MiB of HBM per device.

```python
import math
import jax
import jax.numpy as jnp
from jax import lax

R = 8192
BLOCK = 256
BEAMS = 16
LEVELS = 4
TAPS = 4
SHIFT = 24
SPREAD = 4
PUL_DEV = 8
HOP = 128
PULSES = 128
N_PULSE = 16


def draw_beam_map(key, part):
    jitter = jax.random.randint(key, (LEVELS, 2, 2, BEAMS), -1, 2)
    half_index = jnp.arange(2, dtype=jnp.int32)[None, :, None, None]
    position = jnp.arange(BEAMS, dtype=jnp.int32)[None, None, None, :]
    return jnp.clip(half_index * (BEAMS // 2) + position // 2 + jitter, 0, BEAMS - 1).astype(jnp.int32)


def draw_tap_offsets(key, part):
    rows_list = []
    for level_index in range(LEVELS):
        shuffled = jax.random.permutation(jax.random.fold_in(key, level_index + 17), 2 * SPREAD + 1)
        rows_list.append(shuffled[:TAPS])
    return (jnp.stack(rows_list) - SPREAD).astype(jnp.int32)


def touch_ends(values, key, smallest, top_value):
    index_at = [jax.random.randint(jax.random.fold_in(key, axis), (), 0, length) for axis, length in enumerate(values.shape)]
    main_axis = values.shape.index(max(values.shape))
    beside = index_at[:main_axis] + [(index_at[main_axis] + 1) % values.shape[main_axis]] + index_at[main_axis + 1:]
    return values.at[tuple(index_at)].set(smallest).at[tuple(beside)].set(top_value)


def block_scale(own_key, dims, cuts, least, largest):
    def one(dim, blocks):
        draws = jax.random.uniform(jax.random.fold_in(jax.random.fold_in(own_key, 6), dim), (blocks,), jnp.float32, least / len(cuts), largest / len(cuts))
        return jnp.repeat(jnp.exp(draws), dims[dim] // blocks).reshape((-1,) + (1,) * (len(dims) - dim - 1))

    gain = one(*cuts[0])
    for cut in cuts[1:]:
        gain = gain * one(*cut)
    return gain


def centred(own_key, dims, scale, most, split=(), kind=jnp.bfloat16):
    drawn = jax.random.normal(own_key, dims, jnp.float32) * scale
    if len(split) > 0:
        drawn = block_scale(own_key, dims, split, -0.22, 0.18) * drawn
    return jnp.clip(drawn, min=-most, max=most).astype(kind)


def setup_inputs(seed: int = 0, part: int = 0) -> dict:
    key_list = jax.random.split(jax.random.key(seed), 10)
    part_splits = jax.random.split(jax.random.fold_in(key_list[9], part), 10)
    return {
        "raw_echoes": centred(part_splits[0], (PULSES, R // HOP, 2, HOP), 1.0, 6.0, ((0, 16),)),
        "matched": centred(key_list[1], (2, HOP), (2 * HOP) ** -0.5, 0.375, (), jnp.float32),
        "delays": touch_ends(jax.random.randint(part_splits[2], (PULSES, BEAMS), -SHIFT, SHIFT + 1), jax.random.fold_in(part_splits[2], 1), -SHIFT, SHIFT).astype(jnp.int32),
        "pulse_phase": jnp.clip(jax.random.uniform(part_splits[3], (PULSES, BEAMS), jnp.float32, -3.140625, 3.140625), -3.140625, 3.140625),
        "beam_map": draw_beam_map(jax.random.fold_in(key_list[9], 71), part),
        "range_shift": touch_ends(jax.random.randint(key_list[5], (LEVELS, 2, 2, BEAMS), -SHIFT, SHIFT + 1), jax.random.fold_in(key_list[5], 1), -SHIFT, SHIFT).astype(jnp.int32),
        "phase_base": jnp.clip(jax.random.uniform(key_list[6], (LEVELS, 2, 2, BEAMS), jnp.float32, -3.140625, 3.140625), -3.140625, 3.140625),
        "phase_rate": jnp.clip(jax.random.uniform(key_list[7], (LEVELS, 2, 2, BEAMS), jnp.float32, -4.0, 4.0), -4.0, 4.0),
        "tap_offsets": draw_tap_offsets(jax.random.fold_in(key_list[9], 71), part),
    }


SQRT_HALF = 0.7071067811865476

def tables(length):
    counter = jnp.arange(length, dtype=jnp.int32)
    product = counter[:, None] * counter[None, :] % length
    angles = product.astype(jnp.float32) * (2.0 * math.pi / length)
    cosine = jnp.cos(angles)
    sine_part = jnp.sin(angles)
    forward = jnp.concatenate([jnp.concatenate([cosine, -sine_part], axis=1), jnp.concatenate([sine_part, cosine], axis=1)], axis=0)
    inverse = jnp.concatenate([jnp.concatenate([cosine, sine_part], axis=1), jnp.concatenate([-sine_part, cosine], axis=1)], axis=0)
    return (forward, inverse)

def compress(echoes, tail, matched, forward_exact, forward, inverse_kept):
    pulses, blocks, parts, hop_bins = echoes.shape
    length = 2 * hop_bins
    previous = jnp.concatenate([tail[:, None], echoes[:, :-1]], axis=1)
    windows = jnp.concatenate([previous, echoes], axis=3).reshape(pulses * blocks, parts * length)
    taps_padded = jnp.concatenate([matched, jnp.zeros((2, length - hop_bins), jnp.float32)], axis=1).reshape(1, 2 * length)
    response = jnp.dot(taps_padded, forward_exact, precision=lax.Precision.HIGHEST)[0]
    resp_real = response[:length]
    resp_imag = response[length:]
    spectrum = jnp.dot(windows, forward, preferred_element_type=jnp.float32)
    spec_real = spectrum[:, :length]
    spec_imag = spectrum[:, length:]
    filt_real = spec_real * resp_real - spec_imag * resp_imag
    filt_imag = spec_real * resp_imag + spec_imag * resp_real
    shaped = jnp.concatenate([filt_real, filt_imag], axis=1).astype(jnp.bfloat16)
    restored = jnp.dot(shaped, inverse_kept, preferred_element_type=jnp.float32) * (1.0 / length)
    return restored.astype(jnp.bfloat16).reshape(pulses, blocks, parts, hop_bins)

def kept_columns(inverse, length):
    half = length // 2
    return jnp.concatenate([inverse[:, half:length], inverse[:, length + half:]], axis=1)

def inside_mask(first_cell, out_cells):
    global_cells = first_cell + jnp.arange(out_cells, dtype=jnp.int32)
    return ((global_cells >= 0) & (global_cells < R)).astype(jnp.float32)

def row_slices(rows, starts, width):

    def per_pulse(row, start_row):
        return jax.vmap(lambda start: lax.dynamic_slice_in_dim(row, start, width, 1))(start_row)
    return jax.vmap(per_pulse)(rows, starts)

def project(padded, delay_rows, phase_rows, offset_base, out_cells, first_cell):
    pulses = padded.shape[0]
    beam_count = delay_rows.shape[1]
    group_size = math.gcd(pulses, 4)
    block_count = pulses // group_size

    def accumulate(summed, block_index):
        first_row = block_index * group_size
        pulses_block = lax.dynamic_slice_in_dim(padded, first_row, group_size, 0)
        delay_block = lax.dynamic_slice_in_dim(delay_rows, first_row, group_size, 0)
        phase_block = lax.dynamic_slice_in_dim(phase_rows, first_row, group_size, 0)
        starts = (delay_block + offset_base).astype(jnp.int32)
        gathered = row_slices(pulses_block, starts, out_cells).astype(jnp.float32)
        cosine = jnp.cos(phase_block)[:, :, None]
        sine_part = jnp.sin(phase_block)[:, :, None]
        real_part = gathered[:, :, 0] * cosine - gathered[:, :, 1] * sine_part
        imag_part = gathered[:, :, 0] * sine_part + gathered[:, :, 1] * cosine
        return (summed + jnp.stack([lax.optimization_barrier(jnp.sum(real_part, axis=0)), lax.optimization_barrier(jnp.sum(imag_part, axis=0))]), None)
    summed, unused = lax.scan(accumulate, jnp.zeros((2, beam_count, out_cells), jnp.float32), jnp.arange(block_count, dtype=jnp.int32))
    return summed * inside_mask(first_cell, out_cells) * (1.0 / math.sqrt(pulses))

def tap_weights(tap_values):
    weights = SPREAD + 1.0 - jnp.abs(tap_values).astype(jnp.float32)
    return weights / jnp.sum(weights)

def merge_side(source, beam_rows, offsets, phase_zero, phase_slope, weights, tap_values, offset_base, out_cells, first_cell):
    picked = jnp.take(source, beam_rows, axis=1)
    span = out_cells + 2 * SPREAD
    starts = (offsets + offset_base - SPREAD).astype(jnp.int32)
    windows = jax.vmap(lambda beam_data, start: lax.dynamic_slice_in_dim(beam_data, start, span, 1), in_axes=(1, 0), out_axes=1)(picked, starts)
    summed = jnp.zeros((2, beam_rows.shape[0], out_cells), jnp.float32)
    for tap_index in range(tap_values.shape[0]):
        tap_start = (tap_values[tap_index] + SPREAD).astype(jnp.int32)
        summed = summed + weights[tap_index] * lax.dynamic_slice_in_dim(windows, tap_start, out_cells, 2)
    positions = jnp.arange(out_cells, dtype=jnp.int32)
    global_cells = (first_cell + positions).astype(jnp.float32)
    angle_grid = phase_zero[:, None] + 2.0 * math.pi / R * phase_slope[:, None] * global_cells[None, :]
    cosine = jnp.cos(angle_grid)
    sine_part = jnp.sin(angle_grid)
    return jnp.stack([summed[0] * cosine - summed[1] * sine_part, summed[0] * sine_part + summed[1] * cosine])

def reference(raw_echoes, matched, delays, pulse_phase, beam_map, range_shift, phase_base, phase_rate, tap_offsets):
    forward_exact, inverse_exact = tables(BLOCK)
    forward = forward_exact.astype(jnp.bfloat16)
    inverse_kept = kept_columns(inverse_exact.astype(jnp.bfloat16), BLOCK)

    def initial(device):
        first_row = device * PUL_DEV
        echoes = lax.dynamic_slice_in_dim(raw_echoes, first_row, PUL_DEV, 0)
        delay_rows = lax.dynamic_slice_in_dim(delays, first_row, PUL_DEV, 0)
        phase_rows = lax.dynamic_slice_in_dim(pulse_phase, first_row, PUL_DEV, 0)
        tail = jnp.zeros((PUL_DEV, 2, HOP), jnp.bfloat16)
        compressed = compress(echoes, tail, matched, forward_exact, forward, inverse_kept)
        compressed = jnp.transpose(compressed, (0, 2, 1, 3)).reshape(PUL_DEV, 2, R)
        padded = jnp.pad(compressed, ((0, 0), (0, 0), (SHIFT, SHIFT)))
        return project(padded, delay_rows, phase_rows, SHIFT, R, 0)
    images = lax.map(initial, jnp.arange(N_PULSE, dtype=jnp.int32))
    rim_cells = SHIFT + SPREAD
    for level_index in range(LEVELS):
        stride = 2 ** level_index
        grouped = images.reshape(N_PULSE // (2 * stride), 2, stride, 2, BEAMS, R)
        widths = ((0, 0), (0, 0), (0, 0), (rim_cells, rim_cells))
        lower_half = jnp.pad(grouped[:, 0].reshape(-1, 2, BEAMS, R), widths)
        upper_half = jnp.pad(grouped[:, 1].reshape(-1, 2, BEAMS, R), widths)
        tap_values = tap_offsets[level_index]
        weights = tap_weights(tap_values)
        halves = []
        for side_bit in range(2):

            def merge_pair(pair_data):
                lower_source, upper_source = pair_data
                first_side = merge_side(lower_source, beam_map[level_index, side_bit, 0], range_shift[level_index, side_bit, 0], phase_base[level_index, side_bit, 0], phase_rate[level_index, side_bit, 0], weights, tap_values, rim_cells, R, 0)
                second_side = merge_side(upper_source, beam_map[level_index, side_bit, 1], range_shift[level_index, side_bit, 1], phase_base[level_index, side_bit, 1], phase_rate[level_index, side_bit, 1], weights, tap_values, rim_cells, R, 0)
                return (first_side + second_side) * SQRT_HALF
            merged = lax.map(merge_pair, (lower_half, upper_half))
            halves.append(merged.reshape(N_PULSE // (2 * stride), stride, 2, BEAMS, R))
        images = jnp.stack(halves, axis=1).reshape(N_PULSE, 2, BEAMS, R)
    return jnp.transpose(images, (1, 0, 2, 3)).reshape(2, N_PULSE * BEAMS, R)
```

```python
import functools
import math

import jax
import jax.numpy as jnp
from jax import lax
from jax.experimental import pallas as pl
from jax.experimental.pallas import tpu as pltpu
from jax.sharding import PartitionSpec as P

R = 8192
BLOCK = 256
LEVELS = 4
SHIFT = 24
SPREAD = 4


SQRT_HALF = 0.7071067811865476


def shifted(array, axis, by):
    count = lax.axis_size(axis)
    pairs = [(i, i + by) for i in range(count) if 0 <= i + by < count]
    return lax.ppermute(array, axis, pairs)


def padded_2(block, sides, width):
    for axis, dim in sides:
        count = lax.axis_size(axis)
        forward = [(i, i + 1) for i in range(count - 1)]
        backward = [(target, source) for source, target in forward]
        low = lax.ppermute(
            lax.slice_in_dim(block, block.shape[dim] - width, None, axis=dim), axis, forward
        )
        high = lax.ppermute(lax.slice_in_dim(block, 0, width, axis=dim), axis, backward)
        block = jnp.concatenate([low, block, high], axis=dim)
    return block


def from_partner(block, axis, bit):
    count = lax.axis_size(axis)
    route = []
    for low in range(count):
        high = low | 1 << bit
        if high != low and high < count:
            route += [(low, high), (high, low)]
    return lax.ppermute(block, axis, route)


def tables(length):
    counter = jnp.arange(length, dtype=jnp.int32)
    product = counter[:, None] * counter[None, :] % length
    angles = product.astype(jnp.float32) * (2.0 * math.pi / length)
    cosine = jnp.cos(angles)
    sine_part = jnp.sin(angles)
    forward = jnp.concatenate(
        [
            jnp.concatenate([cosine, -sine_part], axis=1),
            jnp.concatenate([sine_part, cosine], axis=1),
        ],
        axis=0,
    )
    inverse = jnp.concatenate(
        [
            jnp.concatenate([cosine, sine_part], axis=1),
            jnp.concatenate([-sine_part, cosine], axis=1),
        ],
        axis=0,
    )
    return (forward, inverse)


def compress(echoes, tail, matched, forward_exact, forward, inverse_kept):
    pulses, blocks, parts, hop_bins = echoes.shape
    length = 2 * hop_bins
    previous = jnp.concatenate([tail[:, None], echoes[:, :-1]], axis=1)
    windows = jnp.concatenate([previous, echoes], axis=3).reshape(pulses * blocks, parts * length)
    taps_padded = jnp.concatenate(
        [matched, jnp.zeros((2, length - hop_bins), jnp.float32)], axis=1
    ).reshape(1, 2 * length)
    response = jnp.dot(taps_padded, forward_exact, precision=lax.Precision.HIGHEST)[0]
    resp_real = response[:length]
    resp_imag = response[length:]
    spectrum = jnp.dot(windows, forward, preferred_element_type=jnp.float32)
    spec_real = spectrum[:, :length]
    spec_imag = spectrum[:, length:]
    filt_real = spec_real * resp_real - spec_imag * resp_imag
    filt_imag = spec_real * resp_imag + spec_imag * resp_real
    shaped = jnp.concatenate([filt_real, filt_imag], axis=1).astype(jnp.bfloat16)
    restored = jnp.dot(shaped, inverse_kept, preferred_element_type=jnp.float32) * (1.0 / length)
    return restored.astype(jnp.bfloat16).reshape(pulses, blocks, parts, hop_bins)


def kept_columns(inverse, length):
    half = length // 2
    return jnp.concatenate([inverse[:, half:length], inverse[:, length + half :]], axis=1)


def inside_mask(first_cell, out_cells):
    global_cells = first_cell + jnp.arange(out_cells, dtype=jnp.int32)
    return ((global_cells >= 0) & (global_cells < R)).astype(jnp.float32)


def row_slices(rows, starts, width):

    def per_pulse(row, start_row):
        return jax.vmap(lambda start: lax.dynamic_slice_in_dim(row, start, width, 1))(start_row)

    return jax.vmap(per_pulse)(rows, starts)


def project(padded, delay_rows, phase_rows, offset_base, out_cells, first_cell):
    pulses = padded.shape[0]
    beam_count = delay_rows.shape[1]
    group_size = math.gcd(pulses, 4)
    block_count = pulses // group_size

    def accumulate(summed, block_index):
        first_row = block_index * group_size
        pulses_block = lax.dynamic_slice_in_dim(padded, first_row, group_size, 0)
        delay_block = lax.dynamic_slice_in_dim(delay_rows, first_row, group_size, 0)
        phase_block = lax.dynamic_slice_in_dim(phase_rows, first_row, group_size, 0)
        starts = delay_block + offset_base
        gathered = row_slices(pulses_block, starts, out_cells).astype(jnp.float32)
        cosine = jnp.cos(phase_block)[:, :, None]
        sine_part = jnp.sin(phase_block)[:, :, None]
        real_part = gathered[:, :, 0] * cosine - gathered[:, :, 1] * sine_part
        imag_part = gathered[:, :, 0] * sine_part + gathered[:, :, 1] * cosine
        return (summed + jnp.stack([jnp.sum(real_part, axis=0), jnp.sum(imag_part, axis=0)]), None)

    summed, unused = lax.scan(
        accumulate,
        jnp.zeros((2, beam_count, out_cells), jnp.float32),
        jnp.arange(block_count, dtype=jnp.int32),
    )
    return summed * inside_mask(first_cell, out_cells) * (1.0 / math.sqrt(pulses))


def tap_weights(tap_values):
    weights = SPREAD + 1.0 - jnp.abs(tap_values).astype(jnp.float32)
    return weights / jnp.sum(weights)


def merge_side(
    source,
    beam_rows,
    offsets,
    phase_zero,
    phase_slope,
    weights,
    tap_values,
    offset_base,
    out_cells,
    first_cell,
):
    picked = jnp.take(source, beam_rows, axis=1)
    span = out_cells + 2 * SPREAD
    starts = offsets + offset_base - SPREAD
    windows = jax.vmap(
        lambda beam_data, start: lax.dynamic_slice_in_dim(beam_data, start, span, 1),
        in_axes=(1, 0),
        out_axes=1,
    )(picked, starts)
    summed = jnp.zeros((2, beam_rows.shape[0], out_cells), jnp.float32)
    for tap_index in range(tap_values.shape[0]):
        tap_start = tap_values[tap_index] + SPREAD
        summed = summed + weights[tap_index] * lax.dynamic_slice_in_dim(
            windows, tap_start, out_cells, 2
        )
    positions = jnp.arange(out_cells, dtype=jnp.int32)
    global_cells = (first_cell + positions).astype(jnp.float32)
    angle_grid = (
        phase_zero[:, None] + 2.0 * math.pi / R * phase_slope[:, None] * global_cells[None, :]
    )
    cosine = jnp.cos(angle_grid)
    sine_part = jnp.sin(angle_grid)
    return jnp.stack(
        [summed[0] * cosine - summed[1] * sine_part, summed[0] * sine_part + summed[1] * cosine]
    )


def pick_sides(table, level_index, side_bit):
    half_rows = lax.dynamic_index_in_dim(table[level_index], side_bit, 0, keepdims=False)
    own_rows = lax.dynamic_index_in_dim(half_rows, side_bit, 0, keepdims=False)
    other_rows = lax.dynamic_index_in_dim(half_rows, 1 - side_bit, 0, keepdims=False)
    return (own_rows, other_rows)


def local(
    raw_echoes,
    matched,
    delays,
    pulse_phase,
    beam_map,
    range_shift,
    phase_base,
    phase_rate,
    tap_offsets,
):
    pulses = raw_echoes.shape[0]
    hop_bins = raw_echoes.shape[3]
    local_cells = raw_echoes.shape[1] * hop_bins
    forward_exact, inverse_exact = tables(BLOCK)
    forward = forward_exact.astype(jnp.bfloat16)
    inverse_kept = kept_columns(inverse_exact.astype(jnp.bfloat16), BLOCK)
    tail = shifted(raw_echoes[:, -1], "rng", 1)
    compressed = compress(raw_echoes, tail, matched, forward_exact, forward, inverse_kept)
    compressed = jnp.transpose(compressed, (0, 2, 1, 3)).reshape(pulses, 2, local_cells)
    first_cell = lax.axis_index("rng") * local_cells
    rim_cells = SHIFT + SPREAD
    margin_cells = LEVELS * rim_cells
    padded = padded_2(compressed, (("rng", 2),), SHIFT + margin_cells)
    polar_image = project(
        padded,
        delays,
        pulse_phase,
        SHIFT,
        local_cells + 2 * margin_cells,
        first_cell - margin_cells,
    )
    pulse_index = lax.axis_index("pulse")
    for level_index in range(LEVELS):
        side_bit = pulse_index // 2**level_index % 2
        own_beams, other_beams = pick_sides(beam_map, level_index, side_bit)
        own_offsets, other_offsets = pick_sides(range_shift, level_index, side_bit)
        own_zero, other_zero = pick_sides(phase_base, level_index, side_bit)
        own_slope, other_slope = pick_sides(phase_rate, level_index, side_bit)
        tap_values = tap_offsets[level_index]
        weights = tap_weights(tap_values)
        received = from_partner(polar_image, "pulse", level_index)
        own_source = polar_image
        out_margin = max(margin_cells - rim_cells * (level_index + 1), 0)
        out_cells = local_cells + 2 * out_margin
        start_cell = first_cell - out_margin
        own_side = merge_side(
            own_source,
            own_beams,
            own_offsets,
            own_zero,
            own_slope,
            weights,
            tap_values,
            rim_cells,
            out_cells,
            start_cell,
        )
        other_side = merge_side(
            received,
            other_beams,
            other_offsets,
            other_zero,
            other_slope,
            weights,
            tap_values,
            rim_cells,
            out_cells,
            start_cell,
        )
        polar_image = (own_side + other_side) * SQRT_HALF * inside_mask(start_cell, out_cells)
    return polar_image


LANES = 128
EDGE = 32


def flip_parts(value, lane):
    return jnp.where(
        lane % 2 == 0, -pltpu.roll(value, LANES - 1, 1), pltpu.roll(value, 1, 1)
    )


def from_previous(value, lane):
    return jnp.where(lane < 2, 0.0, pltpu.roll(value, 2, 1))


def from_next(value, lane):
    return jnp.where(lane >= LANES - 2, 0.0, pltpu.roll(value, LANES - 2, 1))


def store_extended(target, slot, value):
    rows = value.shape[0]
    lane = lax.broadcasted_iota(jnp.int32, (EDGE, LANES), 1)
    target[slot, EDGE : EDGE + rows, :] = value
    target[slot, 0:EDGE, :] = from_previous(value[rows - EDGE :], lane)
    target[slot, EDGE + rows :, :] = from_next(value[:EDGE], lane)


def kernel(
    pulses,
    beams,
    span,
    echo_ref,
    matched_ref,
    delay_ref,
    trig_ref,
    map_ref,
    shift_ref,
    base_ref,
    rate_ref,
    tap_ref,
    out_ref,
    taps_hold,
    pulse_ext,
    image,
    other,
    filt,
    table,
    partial,
    outgoing,
    incoming,
    turned,
    send_sem,
    recv_sem,
):
    levels = tap_ref.shape[0]
    tap_count = tap_ref.shape[1]
    rows = echo_ref.shape[1]
    me = lax.axis_index("pulse")
    partners = []
    bits = []
    for level in range(levels):
        bit = me // 2**level % 2
        bits.append(bit)
        partners.append(me + (1 - 2 * bit) * 2**level)

    barrier = pltpu.get_barrier_semaphore()
    for partner in partners:
        pl.semaphore_signal(
            barrier, inc=1, device_id={"pulse": partner}, device_id_type=pl.DeviceIdType.MESH
        )

    lane = lax.broadcasted_iota(jnp.int32, (rows, LANES), 1)
    row = lax.broadcasted_iota(jnp.int32, (rows, LANES), 0)

    for part in range(2):
        spread_taps = jnp.broadcast_to(matched_ref[part : part + 1, :], (rows, LANES))
        circulant = jnp.transpose(pltpu.roll(spread_taps, 0, 1, stride=1, stride_axis=0))
        for side in range(2):
            kept = jnp.where((row >= lane) == (side == 0), circulant, 0.0)
            high = kept.astype(jnp.bfloat16)
            low = (kept - high.astype(jnp.float32)).astype(jnp.bfloat16)
            place = (part * 2 + side) * rows
            taps_hold[0, place : place + rows, :] = high
            taps_hold[1, place : place + rows, :] = low

    def compress_pulse(pulse, carry):
        first = pl.multiple_of(pulse * LANES, LANES)
        data = echo_ref[pl.ds(first, LANES), :]

        def times(part, side):
            place = (part * 2 + side) * rows
            dims = (((1,), (1,)), ((), ()))
            return lax.dot_general(
                taps_hold[0, place : place + rows, :], data, dims, preferred_element_type=jnp.float32
            ) + lax.dot_general(
                taps_hold[1, place : place + rows, :], data, dims, preferred_element_type=jnp.float32
            )

        real_taps = times(0, 0) + from_previous(times(0, 1), lane)
        imag_taps = times(1, 0) + from_previous(times(1, 1), lane)
        store_extended(pulse_ext, pulse, real_taps + flip_parts(imag_taps, lane))
        return carry

    lax.fori_loop(0, pulses, compress_pulse, 0)

    def project_beam(beam, carry):
        cos_sum = jnp.zeros((rows, LANES), jnp.float32)
        sin_sum = jnp.zeros((rows, LANES), jnp.float32)
        for pulse in range(pulses):
            slab = pulse_ext[pulse, pl.ds(EDGE + delay_ref[pulse, beam], rows), :]
            cos_sum += trig_ref[0, pulse, beam] * slab
            sin_sum += trig_ref[1, pulse, beam] * slab
        value = cos_sum + flip_parts(sin_sum, lane)
        store_extended(image, beam, value)
        outgoing[0, beam] = value.astype(jnp.bfloat16)
        return carry

    lax.fori_loop(0, beams, project_beam, 0)
    pl.semaphore_wait(barrier, levels)

    small_lane = lax.broadcasted_iota(jnp.int32, (8, LANES), 1)
    small_row = lax.broadcasted_iota(jnp.int32, (8, LANES), 0)
    cells = (small_lane // 2 * rows + small_row).astype(jnp.float32)
    filt_rows = filt.shape[2]
    copies = []
    for level in range(levels):
        bit = bits[level]
        own_first = bit * (beams - span)
        their_first = (1 - bit) * (beams - span)
        copy = pltpu.make_async_remote_copy(
            src_ref=outgoing.at[level, pl.ds(their_first, span)],
            dst_ref=incoming.at[level],
            send_sem=send_sem.at[level],
            recv_sem=recv_sem.at[level],
            device_id={"pulse": partners[level]},
            device_id_type=pl.DeviceIdType.MESH,
        )
        copy.start()
        copies.append(copy)

        raw_weights = [
            jnp.full(
                (8, LANES), SPREAD + 1 - jnp.abs(tap_ref[level, tap]), jnp.int32
            ).astype(jnp.float32)
            for tap in range(tap_count)
        ]
        total = raw_weights[0]
        for weight in raw_weights[1:]:
            total = total + weight
        weights = [
            jnp.tile(weight * SQRT_HALF / total, (filt_rows // 8, 1)) for weight in raw_weights
        ]

        def fill_table(index, carry, level=level, bit=bit):
            side = index // beams
            beam = index % beams
            zero = base_ref[level, bit, side, beam]
            slope = rate_ref[level, bit, side, beam] * (2.0 * math.pi / R)
            angle = zero + slope * cells
            step = jnp.full((8, LANES), slope * 8.0, jnp.float32)
            cosine, sine = jnp.cos(angle), jnp.sin(angle)
            step_cos, step_sin = jnp.cos(step), jnp.sin(step)
            stack = [(cosine, sine)]
            while len(stack) * 8 < rows:
                stack = stack + [
                    (c * step_cos - s * step_sin, s * step_cos + c * step_sin) for c, s in stack
                ]
                step_cos, step_sin = (
                    step_cos * step_cos - step_sin * step_sin,
                    2.0 * step_cos * step_sin,
                )
            for place, (c, s) in enumerate(stack):
                table[0, index, place * 8 : place * 8 + 8, :] = c
                table[1, index, place * 8 : place * 8 + 8, :] = s
            return carry

        lax.fori_loop(0, 2 * beams, fill_table, 0)

        def filter_rows(source, slot, level=level, weights=weights):
            summed = None
            for tap in range(tap_count):
                start = EDGE - SHIFT + tap_ref[level, tap]
                term = weights[tap] * source[slot, pl.ds(start, filt_rows), :]
                summed = term if summed is None else summed + term
            return summed

        def filter_own(index, carry, own_first=own_first, filter_rows=filter_rows):
            filt[0, index] = filter_rows(image, own_first + index)
            return carry

        lax.fori_loop(0, span, filter_own, 0)

        def slab_of(which, side, beam, level=level, bit=bit, own_first=own_first):
            source = jnp.clip(map_ref[level, bit, side, beam] - own_first, 0, span - 1)
            start = SHIFT + shift_ref[level, bit, side, beam]
            return filt[which, source, pl.ds(start, rows), :]

        def merge_own(beam, carry, bit=bit, slab_of=slab_of):
            slab = slab_of(0, bit, beam)
            index = bit * beams + beam
            partial[0, beam] = table[0, index] * slab
            partial[1, beam] = table[1, index] * slab
            return carry

        lax.fori_loop(0, beams, merge_own, 0)
        copy.wait_recv()

        def filter_other(index, carry, level=level, filter_rows=filter_rows):
            store_extended(other, 0, incoming[level, index].astype(jnp.float32))
            filt[1, index] = filter_rows(other, 0)
            return carry

        lax.fori_loop(0, span, filter_other, 0)

        def merge_other(beam, carry, level=level, bit=bit, slab_of=slab_of):
            slab = slab_of(1, 1 - bit, beam)
            index = (1 - bit) * beams + beam
            cos_sum = partial[0, beam] + table[0, index] * slab
            sin_sum = partial[1, beam] + table[1, index] * slab
            value = cos_sum + flip_parts(sin_sum, lane)
            if level + 1 < levels:
                store_extended(image, beam, value)
                outgoing[level + 1, beam] = value.astype(jnp.bfloat16)
            else:
                first = pl.multiple_of(beam * LANES, LANES)
                turned[pl.ds(first, LANES), :] = jnp.transpose(value)
            return carry

        lax.fori_loop(0, beams, merge_other, 0)

    def put_block(block, carry):
        column = pl.multiple_of(block * rows, rows)
        for part in range(2):
            for group in range(beams // 8):
                start = group * 8 * LANES + 2 * block + part
                out_ref[part, group * 8 : group * 8 + 8, pl.ds(column, rows)] = turned[
                    pl.ds(start, 8, stride=LANES), :
                ]
        return carry

    lax.fori_loop(0, LANES // 2, put_block, 0)
    for copy in copies:
        copy.wait_send()


def local_fused(
    raw_echoes,
    matched,
    delays,
    pulse_phase,
    beam_map,
    range_shift,
    phase_base,
    phase_rate,
    tap_offsets,
):
    pulses, blocks, parts, hop_bins = raw_echoes.shape
    beams = delays.shape[1]
    levels = tap_offsets.shape[0]
    span = beams // 2 + 1
    echoes = raw_echoes.reshape(pulses * blocks * parts, hop_bins)
    trig = jnp.stack([jnp.cos(pulse_phase), jnp.sin(pulse_phase)]) * (1.0 / math.sqrt(pulses))
    vmem = pl.BlockSpec(memory_space=pltpu.VMEM)
    smem = pl.BlockSpec(memory_space=pltpu.SMEM)
    extended = hop_bins + 2 * EDGE
    return pl.pallas_call(
        functools.partial(kernel, pulses, beams, span),
        out_shape=jax.ShapeDtypeStruct((parts, beams, blocks * hop_bins), jnp.float32),
        in_specs=[vmem, vmem] + [smem] * 7,
        out_specs=vmem,
        scratch_shapes=[
            pltpu.VMEM((2, 4 * hop_bins, LANES), jnp.bfloat16),
            pltpu.VMEM((pulses, extended, LANES), jnp.float32),
            pltpu.VMEM((beams, extended, LANES), jnp.float32),
            pltpu.VMEM((1, extended, LANES), jnp.float32),
            pltpu.VMEM((2, span, hop_bins + 2 * SHIFT, LANES), jnp.float32),
            pltpu.VMEM((2, 2 * beams, hop_bins, LANES), jnp.float32),
            pltpu.VMEM((2, beams, hop_bins, LANES), jnp.float32),
            pltpu.VMEM((levels, beams, hop_bins, LANES), jnp.bfloat16),
            pltpu.VMEM((levels, span, hop_bins, LANES), jnp.bfloat16),
            pltpu.VMEM((beams * LANES, hop_bins), jnp.float32),
            pltpu.SemaphoreType.DMA((levels,)),
            pltpu.SemaphoreType.DMA((levels,)),
        ],
        compiler_params=pltpu.CompilerParams(
            collective_id=0, has_side_effects=True, vmem_limit_bytes=48 * 2**20
        ),
    )(
        echoes,
        matched,
        delays,
        trig,
        beam_map,
        range_shift,
        phase_base,
        phase_rate,
        tap_offsets,
    )


def local_any(raw_echoes, *rest):
    pulses, blocks, parts, hop_bins = raw_echoes.shape
    paired = lax.axis_size("pulse") % 2**LEVELS == 0
    if lax.axis_size("rng") == 1 and blocks * parts == LANES and hop_bins == LANES and paired:
        return local_fused(raw_echoes, *rest)
    return local(raw_echoes, *rest)


def solution(mesh):
    in_specs = (
        P(("grp", "pulse"), "rng", None, None),
        P(),
        P(("grp", "pulse"), None),
        P(("grp", "pulse"), None),
        P(),
        P(),
        P(),
        P(),
        P(),
    )
    out_specs = P(None, ("grp", "pulse"), "rng")
    return jax.shard_map(local_any, mesh=mesh, in_specs=in_specs, out_specs=out_specs, check_vma=False)
```

```python
import functools
import math

import jax
import jax.numpy as jnp
from jax import lax
from jax.experimental import pallas as pl
from jax.experimental.pallas import tpu as pltpu
from jax.sharding import PartitionSpec as P

R = 8192
BLOCK = 256
LEVELS = 4
SHIFT = 24
SPREAD = 4


SQRT_HALF = 0.7071067811865476


def shifted(array, axis, by):
    count = lax.axis_size(axis)
    pairs = [(i, i + by) for i in range(count) if 0 <= i + by < count]
    return lax.ppermute(array, axis, pairs)


def padded_2(block, sides, width):
    for axis, dim in sides:
        count = lax.axis_size(axis)
        forward = [(i, i + 1) for i in range(count - 1)]
        backward = [(target, source) for source, target in forward]
        low = lax.ppermute(
            lax.slice_in_dim(block, block.shape[dim] - width, None, axis=dim), axis, forward
        )
        high = lax.ppermute(lax.slice_in_dim(block, 0, width, axis=dim), axis, backward)
        block = jnp.concatenate([low, block, high], axis=dim)
    return block


def from_partner(block, axis, bit):
    count = lax.axis_size(axis)
    route = []
    for low in range(count):
        high = low | 1 << bit
        if high != low and high < count:
            route += [(low, high), (high, low)]
    return lax.ppermute(block, axis, route)


def tables(length):
    counter = jnp.arange(length, dtype=jnp.int32)
    product = counter[:, None] * counter[None, :] % length
    angles = product.astype(jnp.float32) * (2.0 * math.pi / length)
    cosine = jnp.cos(angles)
    sine_part = jnp.sin(angles)
    forward = jnp.concatenate(
        [
            jnp.concatenate([cosine, -sine_part], axis=1),
            jnp.concatenate([sine_part, cosine], axis=1),
        ],
        axis=0,
    )
    inverse = jnp.concatenate(
        [
            jnp.concatenate([cosine, sine_part], axis=1),
            jnp.concatenate([-sine_part, cosine], axis=1),
        ],
        axis=0,
    )
    return (forward, inverse)


def compress(echoes, tail, matched, forward_exact, forward, inverse_kept):
    pulses, blocks, parts, hop_bins = echoes.shape
    length = 2 * hop_bins
    previous = jnp.concatenate([tail[:, None], echoes[:, :-1]], axis=1)
    windows = jnp.concatenate([previous, echoes], axis=3).reshape(pulses * blocks, parts * length)
    taps_padded = jnp.concatenate(
        [matched, jnp.zeros((2, length - hop_bins), jnp.float32)], axis=1
    ).reshape(1, 2 * length)
    response = jnp.dot(taps_padded, forward_exact, precision=lax.Precision.HIGHEST)[0]
    resp_real = response[:length]
    resp_imag = response[length:]
    spectrum = jnp.dot(windows, forward, preferred_element_type=jnp.float32)
    spec_real = spectrum[:, :length]
    spec_imag = spectrum[:, length:]
    filt_real = spec_real * resp_real - spec_imag * resp_imag
    filt_imag = spec_real * resp_imag + spec_imag * resp_real
    shaped = jnp.concatenate([filt_real, filt_imag], axis=1).astype(jnp.bfloat16)
    restored = jnp.dot(shaped, inverse_kept, preferred_element_type=jnp.float32) * (1.0 / length)
    return restored.astype(jnp.bfloat16).reshape(pulses, blocks, parts, hop_bins)


def kept_columns(inverse, length):
    half = length // 2
    return jnp.concatenate([inverse[:, half:length], inverse[:, length + half :]], axis=1)


def inside_mask(first_cell, out_cells):
    global_cells = first_cell + jnp.arange(out_cells, dtype=jnp.int32)
    return ((global_cells >= 0) & (global_cells < R)).astype(jnp.float32)


def row_slices(rows, starts, width):

    def per_pulse(row, start_row):
        return jax.vmap(lambda start: lax.dynamic_slice_in_dim(row, start, width, 1))(start_row)

    return jax.vmap(per_pulse)(rows, starts)


def project(padded, delay_rows, phase_rows, offset_base, out_cells, first_cell):
    pulses = padded.shape[0]
    beam_count = delay_rows.shape[1]
    group_size = math.gcd(pulses, 4)
    block_count = pulses // group_size

    def accumulate(summed, block_index):
        first_row = block_index * group_size
        pulses_block = lax.dynamic_slice_in_dim(padded, first_row, group_size, 0)
        delay_block = lax.dynamic_slice_in_dim(delay_rows, first_row, group_size, 0)
        phase_block = lax.dynamic_slice_in_dim(phase_rows, first_row, group_size, 0)
        starts = delay_block + offset_base
        gathered = row_slices(pulses_block, starts, out_cells).astype(jnp.float32)
        cosine = jnp.cos(phase_block)[:, :, None]
        sine_part = jnp.sin(phase_block)[:, :, None]
        real_part = gathered[:, :, 0] * cosine - gathered[:, :, 1] * sine_part
        imag_part = gathered[:, :, 0] * sine_part + gathered[:, :, 1] * cosine
        return (summed + jnp.stack([jnp.sum(real_part, axis=0), jnp.sum(imag_part, axis=0)]), None)

    summed, unused = lax.scan(
        accumulate,
        jnp.zeros((2, beam_count, out_cells), jnp.float32),
        jnp.arange(block_count, dtype=jnp.int32),
    )
    return summed * inside_mask(first_cell, out_cells) * (1.0 / math.sqrt(pulses))


def tap_weights(tap_values):
    weights = SPREAD + 1.0 - jnp.abs(tap_values).astype(jnp.float32)
    return weights / jnp.sum(weights)


def merge_side(
    source,
    beam_rows,
    offsets,
    phase_zero,
    phase_slope,
    weights,
    tap_values,
    offset_base,
    out_cells,
    first_cell,
):
    picked = jnp.take(source, beam_rows, axis=1)
    span = out_cells + 2 * SPREAD
    starts = offsets + offset_base - SPREAD
    windows = jax.vmap(
        lambda beam_data, start: lax.dynamic_slice_in_dim(beam_data, start, span, 1),
        in_axes=(1, 0),
        out_axes=1,
    )(picked, starts)
    summed = jnp.zeros((2, beam_rows.shape[0], out_cells), jnp.float32)
    for tap_index in range(tap_values.shape[0]):
        tap_start = tap_values[tap_index] + SPREAD
        summed = summed + weights[tap_index] * lax.dynamic_slice_in_dim(
            windows, tap_start, out_cells, 2
        )
    positions = jnp.arange(out_cells, dtype=jnp.int32)
    global_cells = (first_cell + positions).astype(jnp.float32)
    angle_grid = (
        phase_zero[:, None] + 2.0 * math.pi / R * phase_slope[:, None] * global_cells[None, :]
    )
    cosine = jnp.cos(angle_grid)
    sine_part = jnp.sin(angle_grid)
    return jnp.stack(
        [summed[0] * cosine - summed[1] * sine_part, summed[0] * sine_part + summed[1] * cosine]
    )


def pick_sides(table, level_index, side_bit):
    half_rows = lax.dynamic_index_in_dim(table[level_index], side_bit, 0, keepdims=False)
    own_rows = lax.dynamic_index_in_dim(half_rows, side_bit, 0, keepdims=False)
    other_rows = lax.dynamic_index_in_dim(half_rows, 1 - side_bit, 0, keepdims=False)
    return (own_rows, other_rows)


def local(
    raw_echoes,
    matched,
    delays,
    pulse_phase,
    beam_map,
    range_shift,
    phase_base,
    phase_rate,
    tap_offsets,
):
    pulses = raw_echoes.shape[0]
    hop_bins = raw_echoes.shape[3]
    local_cells = raw_echoes.shape[1] * hop_bins
    forward_exact, inverse_exact = tables(BLOCK)
    forward = forward_exact.astype(jnp.bfloat16)
    inverse_kept = kept_columns(inverse_exact.astype(jnp.bfloat16), BLOCK)
    tail = shifted(raw_echoes[:, -1], "rng", 1)
    compressed = compress(raw_echoes, tail, matched, forward_exact, forward, inverse_kept)
    compressed = jnp.transpose(compressed, (0, 2, 1, 3)).reshape(pulses, 2, local_cells)
    first_cell = lax.axis_index("rng") * local_cells
    rim_cells = SHIFT + SPREAD
    margin_cells = LEVELS * rim_cells
    padded = padded_2(compressed, (("rng", 2),), SHIFT + margin_cells)
    polar_image = project(
        padded,
        delays,
        pulse_phase,
        SHIFT,
        local_cells + 2 * margin_cells,
        first_cell - margin_cells,
    )
    pulse_index = lax.axis_index("pulse")
    for level_index in range(LEVELS):
        side_bit = pulse_index // 2**level_index % 2
        own_beams, other_beams = pick_sides(beam_map, level_index, side_bit)
        own_offsets, other_offsets = pick_sides(range_shift, level_index, side_bit)
        own_zero, other_zero = pick_sides(phase_base, level_index, side_bit)
        own_slope, other_slope = pick_sides(phase_rate, level_index, side_bit)
        tap_values = tap_offsets[level_index]
        weights = tap_weights(tap_values)
        received = from_partner(polar_image, "pulse", level_index)
        own_source = polar_image
        out_margin = max(margin_cells - rim_cells * (level_index + 1), 0)
        out_cells = local_cells + 2 * out_margin
        start_cell = first_cell - out_margin
        own_side = merge_side(
            own_source,
            own_beams,
            own_offsets,
            own_zero,
            own_slope,
            weights,
            tap_values,
            rim_cells,
            out_cells,
            start_cell,
        )
        other_side = merge_side(
            received,
            other_beams,
            other_offsets,
            other_zero,
            other_slope,
            weights,
            tap_values,
            rim_cells,
            out_cells,
            start_cell,
        )
        polar_image = (own_side + other_side) * SQRT_HALF * inside_mask(start_cell, out_cells)
    return polar_image


LANES = 128
EDGE = 32


def flip_parts(value, lane):
    return jnp.where(
        lane % 2 == 0, -pltpu.roll(value, LANES - 1, 1), pltpu.roll(value, 1, 1)
    )


def from_previous(value, lane):
    return jnp.where(lane < 2, 0.0, pltpu.roll(value, 2, 1))


def from_next(value, lane):
    return jnp.where(lane >= LANES - 2, 0.0, pltpu.roll(value, LANES - 2, 1))


def store_extended(target, slot, value):
    rows = value.shape[0]
    lane = lax.broadcasted_iota(jnp.int32, (EDGE, LANES), 1)
    target[slot, EDGE : EDGE + rows, :] = value
    target[slot, 0:EDGE, :] = from_previous(value[rows - EDGE :], lane)
    target[slot, EDGE + rows :, :] = from_next(value[:EDGE], lane)


def early_plan(beams, span):
    needs = [0] * span
    for low in (0, beams - span):
        for turn in (0, 2):
            for half in (0, 1):
                for position in range(span):
                    beam = low + (position + turn) % span
                    start = 2 if low else 0
                    for step in (-1, 0, 1):
                        child = min(max(beam // 2 + step + half * (beams // 2), 0), beams - 1)
                        place = (child - half * (beams - span) - start) % span
                        needs[position] = max(needs[position], place + 1)
    plan = []
    for position in range(span):
        need = max(needs[: position + 1])
        if plan and plan[-1][0] == need:
            plan[-1] = (need, position + 1)
        else:
            plan.append((need, position + 1))
    return plan


def kernel(
    pulses,
    beams,
    span,
    echo_ref,
    matched_ref,
    delay_ref,
    trig_ref,
    map_ref,
    shift_ref,
    base_ref,
    rate_ref,
    tap_ref,
    out_ref,
    taps_hold,
    pulse_ext,
    image,
    other,
    filt,
    table,
    outgoing,
    incoming,
    turned,
    send_sem,
    recv_sem,
):
    levels = tap_ref.shape[0]
    tap_count = tap_ref.shape[1]
    rows = echo_ref.shape[1]
    me = lax.axis_index("pulse")
    partners = []
    bits = []
    for level in range(levels):
        bit = me // 2**level % 2
        bits.append(bit)
        partners.append(me + (1 - 2 * bit) * 2**level)

    turns = [2 * (1 - bits[level + 1]) for level in range(levels - 1)] + [0]

    barrier = pltpu.get_barrier_semaphore()
    for partner in partners:
        pl.semaphore_signal(
            barrier, inc=1, device_id={"pulse": partner}, device_id_type=pl.DeviceIdType.MESH
        )

    lane = lax.broadcasted_iota(jnp.int32, (rows, LANES), 1)
    row = lax.broadcasted_iota(jnp.int32, (rows, LANES), 0)

    for part in range(2):
        spread_taps = jnp.broadcast_to(matched_ref[part : part + 1, :], (rows, LANES))
        circulant = jnp.transpose(pltpu.roll(spread_taps, 0, 1, stride=1, stride_axis=0))
        for side in range(2):
            kept = jnp.where((row >= lane) == (side == 0), circulant, 0.0)
            high = kept.astype(jnp.bfloat16)
            low = (kept - high.astype(jnp.float32)).astype(jnp.bfloat16)
            place = (part * 2 + side) * rows
            taps_hold[0, place : place + rows, :] = high
            taps_hold[1, place : place + rows, :] = low

    def compress_pulse(pulse, carry):
        first = pl.multiple_of(pulse * LANES, LANES)
        data = echo_ref[pl.ds(first, LANES), :]

        def times(part, side):
            place = (part * 2 + side) * rows
            dims = (((1,), (1,)), ((), ()))
            return lax.dot_general(
                taps_hold[0, place : place + rows, :], data, dims, preferred_element_type=jnp.float32
            ) + lax.dot_general(
                taps_hold[1, place : place + rows, :], data, dims, preferred_element_type=jnp.float32
            )

        real_taps = times(0, 0) + from_previous(times(0, 1), lane)
        imag_taps = times(1, 0) + from_previous(times(1, 1), lane)
        store_extended(pulse_ext, pulse, real_taps + flip_parts(imag_taps, lane))
        return carry

    lax.fori_loop(0, pulses, compress_pulse, 0)

    def beam_at(level, position):
        first = (1 - bits[level]) * (beams - span)
        early = first + lax.rem(position + turns[level], span)
        late = bits[level] * span + position - span
        return early, late

    def transfer(level, position):
        return pltpu.make_async_remote_copy(
            src_ref=outgoing.at[level, position],
            dst_ref=incoming.at[level, position],
            send_sem=send_sem.at[level, position],
            recv_sem=recv_sem.at[level, position],
            device_id={"pulse": partners[level]},
            device_id_type=pl.DeviceIdType.MESH,
        )

    def project_beam(beam):
        cos_sum = jnp.zeros((rows, LANES), jnp.float32)
        sin_sum = jnp.zeros((rows, LANES), jnp.float32)
        for pulse in range(pulses):
            slab = pulse_ext[pulse, pl.ds(EDGE + delay_ref[pulse, beam], rows), :]
            cos_sum += trig_ref[0, pulse, beam] * slab
            sin_sum += trig_ref[1, pulse, beam] * slab
        return cos_sum + flip_parts(sin_sum, lane)

    def produce(level, make, low, high):
        def step(position, carry):
            early, late = beam_at(level, position)
            beam = early if high <= span else late
            value = make(beam)
            if high <= span:
                outgoing[level, position] = value.astype(jnp.bfloat16)
                transfer(level, position).start()
            store_extended(image, beam, value)
            return carry

        lax.fori_loop(low, high, step, 0)

    pl.semaphore_wait(barrier, levels)
    produce(0, project_beam, 0, span)
    produce(0, project_beam, span, beams)

    small_lane = lax.broadcasted_iota(jnp.int32, (8, LANES), 1)
    small_row = lax.broadcasted_iota(jnp.int32, (8, LANES), 0)
    cells = (small_lane // 2 * rows + small_row).astype(jnp.float32)
    filt_rows = filt.shape[2]
    for level in range(levels):
        bit = bits[level]
        own_first = bit * (beams - span)

        raw_weights = [
            jnp.full(
                (8, LANES), SPREAD + 1 - jnp.abs(tap_ref[level, tap]), jnp.int32
            ).astype(jnp.float32)
            for tap in range(tap_count)
        ]
        total = raw_weights[0]
        for weight in raw_weights[1:]:
            total = total + weight
        weights = [
            jnp.tile(weight * SQRT_HALF / total, (filt_rows // 8, 1)) for weight in raw_weights
        ]

        def fill_one(side, beam, level=level, bit=bit):
            index = side * beams + beam
            zero = base_ref[level, bit, side, beam]
            slope = rate_ref[level, bit, side, beam] * (2.0 * math.pi / R)
            angle = zero + slope * cells
            step = jnp.full((8, LANES), slope * 8.0, jnp.float32)
            cosine, sine = jnp.cos(angle), jnp.sin(angle)
            step_cos, step_sin = jnp.cos(step), jnp.sin(step)
            stack = [(cosine, sine)]
            while len(stack) * 8 < rows:
                stack = stack + [
                    (c * step_cos - s * step_sin, s * step_cos + c * step_sin) for c, s in stack
                ]
                step_cos, step_sin = (
                    step_cos * step_cos - step_sin * step_sin,
                    2.0 * step_cos * step_sin,
                )
            for place, (c, s) in enumerate(stack):
                table[0, index, place * 8 : place * 8 + 8, :] = c
                table[1, index, place * 8 : place * 8 + 8, :] = s

        def fill_table(beam, carry, fill_one=fill_one):
            fill_one(0, beam)
            fill_one(1, beam)
            return carry

        def filter_rows(source, slot, level=level, weights=weights):
            summed = None
            for tap in range(tap_count):
                start = EDGE - SHIFT + tap_ref[level, tap]
                term = weights[tap] * source[slot, pl.ds(start, filt_rows), :]
                summed = term if summed is None else summed + term
            return summed

        def filter_own(index, carry, own_first=own_first, filter_rows=filter_rows):
            filt[0, index] = filter_rows(image, own_first + index)
            return carry

        def filter_other(position, carry, level=level, filter_rows=filter_rows):
            transfer(level, position).wait_recv()
            place = lax.rem(position + turns[level], span)
            store_extended(other, 0, incoming[level, position].astype(jnp.float32))
            filt[1, place] = filter_rows(other, 0)
            return carry

        def slab_of(which, side, beam, level=level, bit=bit, own_first=own_first):
            source = jnp.clip(map_ref[level, bit, side, beam] - own_first, 0, span - 1)
            start = SHIFT + shift_ref[level, bit, side, beam]
            return filt[which, source, pl.ds(start, rows), :]

        def merge(beam, bit=bit, slab_of=slab_of):
            own_slab, own_index = slab_of(0, bit, beam), bit * beams + beam
            other_slab, other_index = slab_of(1, 1 - bit, beam), (1 - bit) * beams + beam
            cos_sum = table[0, own_index] * own_slab + table[0, other_index] * other_slab
            sin_sum = table[1, own_index] * own_slab + table[1, other_index] * other_slab
            return cos_sum + flip_parts(sin_sum, lane)

        def finish(beam, carry, merge=merge):
            first = pl.multiple_of(beam * LANES, LANES)
            turned[pl.ds(first, LANES), :] = jnp.transpose(merge(beam))
            return carry

        lax.fori_loop(0, span, filter_own, 0)
        lax.fori_loop(0, beams, fill_table, 0)
        arrived = 0
        if level + 1 < levels:
            made = 0
            for count, until in early_plan(beams, span):
                lax.fori_loop(arrived, count, filter_other, 0)
                produce(level + 1, merge, made, until)
                arrived, made = count, until
            lax.fori_loop(arrived, span, filter_other, 0)
            produce(level + 1, merge, span, beams)
        else:
            lax.fori_loop(0, 2, filter_other, 0)

            def child_then_pair(position, carry, filter_other=filter_other, finish=finish):
                filter_other(position, 0)
                return lax.fori_loop(2 * position - 4, 2 * position - 2, finish, carry)

            lax.fori_loop(2, span, child_then_pair, 0)
            lax.fori_loop(2 * span - 4, beams, finish, 0)

    def put_block(block, carry):
        column = pl.multiple_of(block * rows, rows)
        for part in range(2):
            for group in range(beams // 8):
                start = group * 8 * LANES + 2 * block + part
                out_ref[part, group * 8 : group * 8 + 8, pl.ds(column, rows)] = turned[
                    pl.ds(start, 8, stride=LANES), :
                ]
        return carry

    lax.fori_loop(0, LANES // 2, put_block, 0)

    def drain(position, carry):
        for level in range(levels):
            transfer(level, position).wait_send()
        return carry

    lax.fori_loop(0, span, drain, 0)


def local_fused(
    raw_echoes,
    matched,
    delays,
    pulse_phase,
    beam_map,
    range_shift,
    phase_base,
    phase_rate,
    tap_offsets,
):
    pulses, blocks, parts, hop_bins = raw_echoes.shape
    beams = delays.shape[1]
    levels = tap_offsets.shape[0]
    span = beams // 2 + 1
    echoes = raw_echoes.reshape(pulses * blocks * parts, hop_bins)
    trig = jnp.stack([jnp.cos(pulse_phase), jnp.sin(pulse_phase)]) * (1.0 / math.sqrt(pulses))
    vmem = pl.BlockSpec(memory_space=pltpu.VMEM)
    smem = pl.BlockSpec(memory_space=pltpu.SMEM)
    extended = hop_bins + 2 * EDGE
    return pl.pallas_call(
        functools.partial(kernel, pulses, beams, span),
        out_shape=jax.ShapeDtypeStruct((parts, beams, blocks * hop_bins), jnp.float32),
        in_specs=[vmem, vmem] + [smem] * 7,
        out_specs=vmem,
        scratch_shapes=[
            pltpu.VMEM((2, 4 * hop_bins, LANES), jnp.bfloat16),
            pltpu.VMEM((pulses, extended, LANES), jnp.float32),
            pltpu.VMEM((beams, extended, LANES), jnp.float32),
            pltpu.VMEM((1, extended, LANES), jnp.float32),
            pltpu.VMEM((2, span, hop_bins + 2 * SHIFT, LANES), jnp.float32),
            pltpu.VMEM((2, 2 * beams, hop_bins, LANES), jnp.float32),
            pltpu.VMEM((levels, span, hop_bins, LANES), jnp.bfloat16),
            pltpu.VMEM((levels, span, hop_bins, LANES), jnp.bfloat16),
            pltpu.VMEM((beams * LANES, hop_bins), jnp.float32),
            pltpu.SemaphoreType.DMA((levels, span)),
            pltpu.SemaphoreType.DMA((levels, span)),
        ],
        compiler_params=pltpu.CompilerParams(
            collective_id=0, has_side_effects=True, vmem_limit_bytes=48 * 2**20
        ),
    )(
        echoes,
        matched,
        delays,
        trig,
        beam_map,
        range_shift,
        phase_base,
        phase_rate,
        tap_offsets,
    )


def local_any(raw_echoes, *rest):
    pulses, blocks, parts, hop_bins = raw_echoes.shape
    paired = lax.axis_size("pulse") % 2**LEVELS == 0
    if lax.axis_size("rng") == 1 and blocks * parts == LANES and hop_bins == LANES and paired:
        return local_fused(raw_echoes, *rest)
    return local(raw_echoes, *rest)


def solution(mesh):
    in_specs = (
        P(("grp", "pulse"), "rng", None, None),
        P(),
        P(("grp", "pulse"), None),
        P(("grp", "pulse"), None),
        P(),
        P(),
        P(),
        P(),
        P(),
    )
    out_specs = P(None, ("grp", "pulse"), "rng")
    return jax.shard_map(local_any, mesh=mesh, in_specs=in_specs, out_specs=out_specs, check_vma=False)
```

```python
import functools
import math

import jax
import jax.numpy as jnp
from jax import lax
from jax.experimental import pallas as pl
from jax.experimental.pallas import tpu as pltpu
from jax.sharding import PartitionSpec as P

R = 8192
BLOCK = 256
LEVELS = 4
SHIFT = 24
SPREAD = 4


SQRT_HALF = 0.7071067811865476


def shifted(array, axis, by):
    count = lax.axis_size(axis)
    pairs = [(i, i + by) for i in range(count) if 0 <= i + by < count]
    return lax.ppermute(array, axis, pairs)


def padded_2(block, sides, width):
    for axis, dim in sides:
        count = lax.axis_size(axis)
        forward = [(i, i + 1) for i in range(count - 1)]
        backward = [(target, source) for source, target in forward]
        low = lax.ppermute(
            lax.slice_in_dim(block, block.shape[dim] - width, None, axis=dim), axis, forward
        )
        high = lax.ppermute(lax.slice_in_dim(block, 0, width, axis=dim), axis, backward)
        block = jnp.concatenate([low, block, high], axis=dim)
    return block


def from_partner(block, axis, bit):
    count = lax.axis_size(axis)
    route = []
    for low in range(count):
        high = low | 1 << bit
        if high != low and high < count:
            route += [(low, high), (high, low)]
    return lax.ppermute(block, axis, route)


def tables(length):
    counter = jnp.arange(length, dtype=jnp.int32)
    product = counter[:, None] * counter[None, :] % length
    angles = product.astype(jnp.float32) * (2.0 * math.pi / length)
    cosine = jnp.cos(angles)
    sine_part = jnp.sin(angles)
    forward = jnp.concatenate(
        [
            jnp.concatenate([cosine, -sine_part], axis=1),
            jnp.concatenate([sine_part, cosine], axis=1),
        ],
        axis=0,
    )
    inverse = jnp.concatenate(
        [
            jnp.concatenate([cosine, sine_part], axis=1),
            jnp.concatenate([-sine_part, cosine], axis=1),
        ],
        axis=0,
    )
    return (forward, inverse)


def compress(echoes, tail, matched, forward_exact, forward, inverse_kept):
    pulses, blocks, parts, hop_bins = echoes.shape
    length = 2 * hop_bins
    previous = jnp.concatenate([tail[:, None], echoes[:, :-1]], axis=1)
    windows = jnp.concatenate([previous, echoes], axis=3).reshape(pulses * blocks, parts * length)
    taps_padded = jnp.concatenate(
        [matched, jnp.zeros((2, length - hop_bins), jnp.float32)], axis=1
    ).reshape(1, 2 * length)
    response = jnp.dot(taps_padded, forward_exact, precision=lax.Precision.HIGHEST)[0]
    resp_real = response[:length]
    resp_imag = response[length:]
    spectrum = jnp.dot(windows, forward, preferred_element_type=jnp.float32)
    spec_real = spectrum[:, :length]
    spec_imag = spectrum[:, length:]
    filt_real = spec_real * resp_real - spec_imag * resp_imag
    filt_imag = spec_real * resp_imag + spec_imag * resp_real
    shaped = jnp.concatenate([filt_real, filt_imag], axis=1).astype(jnp.bfloat16)
    restored = jnp.dot(shaped, inverse_kept, preferred_element_type=jnp.float32) * (1.0 / length)
    return restored.astype(jnp.bfloat16).reshape(pulses, blocks, parts, hop_bins)


def kept_columns(inverse, length):
    half = length // 2
    return jnp.concatenate([inverse[:, half:length], inverse[:, length + half :]], axis=1)


def inside_mask(first_cell, out_cells):
    global_cells = first_cell + jnp.arange(out_cells, dtype=jnp.int32)
    return ((global_cells >= 0) & (global_cells < R)).astype(jnp.float32)


def row_slices(rows, starts, width):

    def per_pulse(row, start_row):
        return jax.vmap(lambda start: lax.dynamic_slice_in_dim(row, start, width, 1))(start_row)

    return jax.vmap(per_pulse)(rows, starts)


def project(padded, delay_rows, phase_rows, offset_base, out_cells, first_cell):
    pulses = padded.shape[0]
    beam_count = delay_rows.shape[1]
    group_size = math.gcd(pulses, 4)
    block_count = pulses // group_size

    def accumulate(summed, block_index):
        first_row = block_index * group_size
        pulses_block = lax.dynamic_slice_in_dim(padded, first_row, group_size, 0)
        delay_block = lax.dynamic_slice_in_dim(delay_rows, first_row, group_size, 0)
        phase_block = lax.dynamic_slice_in_dim(phase_rows, first_row, group_size, 0)
        starts = delay_block + offset_base
        gathered = row_slices(pulses_block, starts, out_cells).astype(jnp.float32)
        cosine = jnp.cos(phase_block)[:, :, None]
        sine_part = jnp.sin(phase_block)[:, :, None]
        real_part = gathered[:, :, 0] * cosine - gathered[:, :, 1] * sine_part
        imag_part = gathered[:, :, 0] * sine_part + gathered[:, :, 1] * cosine
        return (summed + jnp.stack([jnp.sum(real_part, axis=0), jnp.sum(imag_part, axis=0)]), None)

    summed, unused = lax.scan(
        accumulate,
        jnp.zeros((2, beam_count, out_cells), jnp.float32),
        jnp.arange(block_count, dtype=jnp.int32),
    )
    return summed * inside_mask(first_cell, out_cells) * (1.0 / math.sqrt(pulses))


def tap_weights(tap_values):
    weights = SPREAD + 1.0 - jnp.abs(tap_values).astype(jnp.float32)
    return weights / jnp.sum(weights)


def merge_side(
    source,
    beam_rows,
    offsets,
    phase_zero,
    phase_slope,
    weights,
    tap_values,
    offset_base,
    out_cells,
    first_cell,
):
    picked = jnp.take(source, beam_rows, axis=1)
    span = out_cells + 2 * SPREAD
    starts = offsets + offset_base - SPREAD
    windows = jax.vmap(
        lambda beam_data, start: lax.dynamic_slice_in_dim(beam_data, start, span, 1),
        in_axes=(1, 0),
        out_axes=1,
    )(picked, starts)
    summed = jnp.zeros((2, beam_rows.shape[0], out_cells), jnp.float32)
    for tap_index in range(tap_values.shape[0]):
        tap_start = tap_values[tap_index] + SPREAD
        summed = summed + weights[tap_index] * lax.dynamic_slice_in_dim(
            windows, tap_start, out_cells, 2
        )
    positions = jnp.arange(out_cells, dtype=jnp.int32)
    global_cells = (first_cell + positions).astype(jnp.float32)
    angle_grid = (
        phase_zero[:, None] + 2.0 * math.pi / R * phase_slope[:, None] * global_cells[None, :]
    )
    cosine = jnp.cos(angle_grid)
    sine_part = jnp.sin(angle_grid)
    return jnp.stack(
        [summed[0] * cosine - summed[1] * sine_part, summed[0] * sine_part + summed[1] * cosine]
    )


def pick_sides(table, level_index, side_bit):
    half_rows = lax.dynamic_index_in_dim(table[level_index], side_bit, 0, keepdims=False)
    own_rows = lax.dynamic_index_in_dim(half_rows, side_bit, 0, keepdims=False)
    other_rows = lax.dynamic_index_in_dim(half_rows, 1 - side_bit, 0, keepdims=False)
    return (own_rows, other_rows)


def local(
    raw_echoes,
    matched,
    delays,
    pulse_phase,
    beam_map,
    range_shift,
    phase_base,
    phase_rate,
    tap_offsets,
):
    pulses = raw_echoes.shape[0]
    hop_bins = raw_echoes.shape[3]
    local_cells = raw_echoes.shape[1] * hop_bins
    forward_exact, inverse_exact = tables(BLOCK)
    forward = forward_exact.astype(jnp.bfloat16)
    inverse_kept = kept_columns(inverse_exact.astype(jnp.bfloat16), BLOCK)
    tail = shifted(raw_echoes[:, -1], "rng", 1)
    compressed = compress(raw_echoes, tail, matched, forward_exact, forward, inverse_kept)
    compressed = jnp.transpose(compressed, (0, 2, 1, 3)).reshape(pulses, 2, local_cells)
    first_cell = lax.axis_index("rng") * local_cells
    rim_cells = SHIFT + SPREAD
    margin_cells = LEVELS * rim_cells
    padded = padded_2(compressed, (("rng", 2),), SHIFT + margin_cells)
    polar_image = project(
        padded,
        delays,
        pulse_phase,
        SHIFT,
        local_cells + 2 * margin_cells,
        first_cell - margin_cells,
    )
    pulse_index = lax.axis_index("pulse")
    for level_index in range(LEVELS):
        side_bit = pulse_index // 2**level_index % 2
        own_beams, other_beams = pick_sides(beam_map, level_index, side_bit)
        own_offsets, other_offsets = pick_sides(range_shift, level_index, side_bit)
        own_zero, other_zero = pick_sides(phase_base, level_index, side_bit)
        own_slope, other_slope = pick_sides(phase_rate, level_index, side_bit)
        tap_values = tap_offsets[level_index]
        weights = tap_weights(tap_values)
        received = from_partner(polar_image, "pulse", level_index)
        own_source = polar_image
        out_margin = max(margin_cells - rim_cells * (level_index + 1), 0)
        out_cells = local_cells + 2 * out_margin
        start_cell = first_cell - out_margin
        own_side = merge_side(
            own_source,
            own_beams,
            own_offsets,
            own_zero,
            own_slope,
            weights,
            tap_values,
            rim_cells,
            out_cells,
            start_cell,
        )
        other_side = merge_side(
            received,
            other_beams,
            other_offsets,
            other_zero,
            other_slope,
            weights,
            tap_values,
            rim_cells,
            out_cells,
            start_cell,
        )
        polar_image = (own_side + other_side) * SQRT_HALF * inside_mask(start_cell, out_cells)
    return polar_image


LANES = 128
EDGE = 32


def flip_parts(value, lane):
    return jnp.where(
        lane % 2 == 0, -pltpu.roll(value, LANES - 1, 1), pltpu.roll(value, 1, 1)
    )


def from_previous(value, lane):
    return jnp.where(lane < 2, 0.0, pltpu.roll(value, 2, 1))


def from_next(value, lane):
    return jnp.where(lane >= LANES - 2, 0.0, pltpu.roll(value, LANES - 2, 1))


def store_extended(target, slot, value):
    rows = value.shape[0]
    lane = lax.broadcasted_iota(jnp.int32, (EDGE, LANES), 1)
    target[slot, EDGE : EDGE + rows, :] = value
    target[slot, 0:EDGE, :] = from_previous(value[rows - EDGE :], lane)
    target[slot, EDGE + rows :, :] = from_next(value[:EDGE], lane)


def sin_cos(turns):
    half_turns = jnp.floor(2.0 * turns + 0.5)
    angle = (turns - 0.5 * half_turns) * (2.0 * math.pi)
    sign = 1.0 - 2.0 * (half_turns - 2.0 * jnp.floor(0.5 * half_turns))
    square = angle * angle
    sine = jnp.full_like(angle, -1.0 / math.factorial(11))
    cosine = jnp.full_like(angle, 1.0 / math.factorial(12))
    for power in (9, 7, 5, 3, 1):
        sine = sine * square + (-1.0) ** (power // 2) / math.factorial(power)
    for power in (10, 8, 6, 4, 2, 0):
        cosine = cosine * square + (-1.0) ** (power // 2) / math.factorial(power)
    return sign * angle * sine, sign * cosine


def early_plan(beams, span):
    needs = [0] * span
    for low in (0, beams - span):
        for turn in (0, 2):
            for half in (0, 1):
                for position in range(span):
                    beam = low + (position + turn) % span
                    start = 2 if low else 0
                    for step in (-1, 0, 1):
                        child = min(max(beam // 2 + step + half * (beams // 2), 0), beams - 1)
                        place = (child - half * (beams - span) - start) % span
                        needs[position] = max(needs[position], place + 1)
    plan = []
    for position in range(span):
        need = max(needs[: position + 1])
        if plan and plan[-1][0] == need:
            plan[-1] = (need, position + 1)
        else:
            plan.append((need, position + 1))
    return plan


def kernel(
    pulses,
    beams,
    span,
    *refs,
):
    sources, (out_ref,), held, work = refs[:9], refs[9:10], refs[10:20], refs[20:]
    (
        echo_ref,
        matched_ref,
        phase_ref,
        delay_ref,
        map_ref,
        shift_ref,
        base_ref,
        rate_ref,
        tap_ref,
        load_sem,
    ) = held
    (
    trig_hold,
    trig_ref,
    trig_sem,
    taps_hold,
    pulse_ext,
    image,
    other,
    filt,
    table,
    outgoing,
    incoming,
    turned,
    send_sem,
    recv_sem,
    ) = work
    loads = [
        pltpu.make_async_copy(source, target, load_sem.at[place])
        for place, (source, target) in enumerate(zip(sources, held))
    ]
    for place in (2, 1, 0, 3, 4, 5, 6, 7, 8):
        loads[place].start()
    levels = tap_ref.shape[0]
    tap_count = tap_ref.shape[1]
    rows = echo_ref.shape[1]
    me = lax.axis_index("pulse")
    partners = []
    bits = []
    for level in range(levels):
        bit = me // 2**level % 2
        bits.append(bit)
        partners.append(me + (1 - 2 * bit) * 2**level)

    turns = [2 * (1 - bits[level + 1]) for level in range(levels - 1)] + [0]

    barrier = pltpu.get_barrier_semaphore()
    for partner in partners:
        pl.semaphore_signal(
            barrier, inc=1, device_id={"pulse": partner}, device_id_type=pl.DeviceIdType.MESH
        )

    lane = lax.broadcasted_iota(jnp.int32, (rows, LANES), 1)
    row = lax.broadcasted_iota(jnp.int32, (rows, LANES), 0)

    loads[2].wait()
    sine, cosine = sin_cos(phase_ref[...] * (0.5 / math.pi))
    trig_hold[0] = cosine * (1.0 / math.sqrt(pulses))
    trig_hold[1] = sine * (1.0 / math.sqrt(pulses))
    to_scalars = pltpu.make_async_copy(trig_hold, trig_ref, trig_sem)
    to_scalars.start()
    loads[1].wait()

    for part in range(2):
        spread_taps = jnp.broadcast_to(matched_ref[part : part + 1, :], (rows, LANES))
        circulant = jnp.transpose(pltpu.roll(spread_taps, 0, 1, stride=1, stride_axis=0))
        for side in range(2):
            kept = jnp.where((row >= lane) == (side == 0), circulant, 0.0)
            high = kept.astype(jnp.bfloat16)
            low = (kept - high.astype(jnp.float32)).astype(jnp.bfloat16)
            place = (part * 2 + side) * rows
            taps_hold[0, place : place + rows, :] = high
            taps_hold[1, place : place + rows, :] = low

    def compress_pulse(pulse, carry):
        first = pl.multiple_of(pulse * LANES, LANES)
        data = echo_ref[pl.ds(first, LANES), :]

        def times(part, side):
            place = (part * 2 + side) * rows
            dims = (((1,), (1,)), ((), ()))
            return lax.dot_general(
                taps_hold[0, place : place + rows, :], data, dims, preferred_element_type=jnp.float32
            ) + lax.dot_general(
                taps_hold[1, place : place + rows, :], data, dims, preferred_element_type=jnp.float32
            )

        real_taps = times(0, 0) + from_previous(times(0, 1), lane)
        imag_taps = times(1, 0) + from_previous(times(1, 1), lane)
        store_extended(pulse_ext, pulse, real_taps + flip_parts(imag_taps, lane))
        return carry

    loads[0].wait()
    lax.fori_loop(0, pulses, compress_pulse, 0)
    for load in loads[3:]:
        load.wait()
    to_scalars.wait()

    def beam_at(level, position):
        first = (1 - bits[level]) * (beams - span)
        early = first + lax.rem(position + turns[level], span)
        late = bits[level] * span + position - span
        return early, late

    def transfer(level, position):
        return pltpu.make_async_remote_copy(
            src_ref=outgoing.at[level, position],
            dst_ref=incoming.at[level, position],
            send_sem=send_sem.at[level, position],
            recv_sem=recv_sem.at[level, position],
            device_id={"pulse": partners[level]},
            device_id_type=pl.DeviceIdType.MESH,
        )

    def project_beam(beam):
        cos_sum = jnp.zeros((rows, LANES), jnp.float32)
        sin_sum = jnp.zeros((rows, LANES), jnp.float32)
        for pulse in range(pulses):
            slab = pulse_ext[pulse, pl.ds(EDGE + delay_ref[pulse, beam], rows), :]
            cos_sum += trig_ref[0, pulse, beam] * slab
            sin_sum += trig_ref[1, pulse, beam] * slab
        return cos_sum + flip_parts(sin_sum, lane)

    def produce(level, make, low, high):
        def step(position, carry):
            early, late = beam_at(level, position)
            beam = early if high <= span else late
            value = make(beam)
            if high <= span:
                outgoing[level, position] = value.astype(jnp.bfloat16)
                transfer(level, position).start()
            store_extended(image, beam, value)
            return carry

        lax.fori_loop(low, high, step, 0)

    def put_group(group):
        def put_block(block, carry):
            column = pl.multiple_of(block * rows, rows)
            for part in range(2):
                start = group * 8 * LANES + 2 * block + part
                out_ref[part, group * 8 : group * 8 + 8, pl.ds(column, rows)] = turned[
                    pl.ds(start, 8, stride=LANES), :
                ]
            return carry

        lax.fori_loop(0, LANES // 2, put_block, 0, unroll=4)

    pl.semaphore_wait(barrier, levels)
    produce(0, project_beam, 0, span)
    produce(0, project_beam, span, beams)

    small_lane = lax.broadcasted_iota(jnp.int32, (8, LANES), 1)
    small_row = lax.broadcasted_iota(jnp.int32, (8, LANES), 0)
    cells = (small_lane // 2 * rows + small_row).astype(jnp.float32)
    filt_rows = filt.shape[2]
    for level in range(levels):
        bit = bits[level]
        own_first = bit * (beams - span)

        raw_weights = [
            jnp.full(
                (8, LANES), SPREAD + 1 - jnp.abs(tap_ref[level, tap]), jnp.int32
            ).astype(jnp.float32)
            for tap in range(tap_count)
        ]
        total = raw_weights[0]
        for weight in raw_weights[1:]:
            total = total + weight
        weights = [
            jnp.tile(weight * SQRT_HALF / total, (filt_rows // 8, 1)) for weight in raw_weights
        ]

        def fill_one(side, beam, level=level, bit=bit):
            index = side * beams + beam
            zero = base_ref[level, bit, side, beam] * (0.5 / math.pi)
            slope = rate_ref[level, bit, side, beam] * (1.0 / R)
            sine, cosine = sin_cos(zero + slope * cells)
            step_sin, step_cos = sin_cos(jnp.full((8, LANES), slope * 8.0, jnp.float32))
            stack = [(cosine, sine)]
            while len(stack) * 8 < rows:
                stack = stack + [
                    (c * step_cos - s * step_sin, s * step_cos + c * step_sin) for c, s in stack
                ]
                step_cos, step_sin = (
                    step_cos * step_cos - step_sin * step_sin,
                    2.0 * step_cos * step_sin,
                )
            for place, (c, s) in enumerate(stack):
                table[0, index, place * 8 : place * 8 + 8, :] = c
                table[1, index, place * 8 : place * 8 + 8, :] = s

        def fill_table(beam, carry, fill_one=fill_one):
            fill_one(0, beam)
            fill_one(1, beam)
            return carry

        def filter_rows(source, slot, level=level, weights=weights):
            summed = None
            for tap in range(tap_count):
                start = EDGE - SHIFT + tap_ref[level, tap]
                term = weights[tap] * source[slot, pl.ds(start, filt_rows), :]
                summed = term if summed is None else summed + term
            return summed

        def filter_own(index, carry, own_first=own_first, filter_rows=filter_rows):
            filt[0, index] = filter_rows(image, own_first + index)
            return carry

        def filter_other(position, carry, level=level, filter_rows=filter_rows):
            transfer(level, position).wait_recv()
            place = lax.rem(position + turns[level], span)
            store_extended(other, 0, incoming[level, position].astype(jnp.float32))
            filt[1, place] = filter_rows(other, 0)
            return carry

        def slab_of(which, side, beam, level=level, bit=bit, own_first=own_first):
            source = jnp.clip(map_ref[level, bit, side, beam] - own_first, 0, span - 1)
            start = SHIFT + shift_ref[level, bit, side, beam]
            return filt[which, source, pl.ds(start, rows), :]

        def merge(beam, bit=bit, slab_of=slab_of):
            own_slab, own_index = slab_of(0, bit, beam), bit * beams + beam
            other_slab, other_index = slab_of(1, 1 - bit, beam), (1 - bit) * beams + beam
            cos_sum = table[0, own_index] * own_slab + table[0, other_index] * other_slab
            sin_sum = table[1, own_index] * own_slab + table[1, other_index] * other_slab
            return cos_sum + flip_parts(sin_sum, lane)

        def finish(beam, carry, merge=merge):
            first = pl.multiple_of(beam * LANES, LANES)
            turned[pl.ds(first, LANES), :] = jnp.transpose(merge(beam))
            return carry

        lax.fori_loop(0, span, filter_own, 0)
        lax.fori_loop(0, beams, fill_table, 0)
        arrived = 0
        if level + 1 < levels:
            made = 0
            for count, until in early_plan(beams, span):
                lax.fori_loop(arrived, count, filter_other, 0)
                produce(level + 1, merge, made, until)
                arrived, made = count, until
            lax.fori_loop(arrived, span, filter_other, 0)
            produce(level + 1, merge, span, beams)
        else:
            lax.fori_loop(0, 2, filter_other, 0)

            def child_then_pair(position, carry, filter_other=filter_other, finish=finish):
                filter_other(position, 0)
                return lax.fori_loop(2 * position - 4, 2 * position - 2, finish, carry)

            done = 2
            for group in range(beams // 8):
                until = min(4 * group + 6, span)
                lax.fori_loop(done, until, child_then_pair, 0)
                lax.fori_loop(2 * until - 4, 8 * group + 8, finish, 0)
                put_group(group)
                done = until

    def drain(position, carry):
        for level in range(levels):
            transfer(level, position).wait_send()
        return carry

    lax.fori_loop(0, span, drain, 0)


def local_fused(
    raw_echoes,
    matched,
    delays,
    pulse_phase,
    beam_map,
    range_shift,
    phase_base,
    phase_rate,
    tap_offsets,
):
    pulses, blocks, parts, hop_bins = raw_echoes.shape
    beams = delays.shape[1]
    levels = tap_offsets.shape[0]
    span = beams // 2 + 1
    echoes = raw_echoes.reshape(pulses * blocks * parts, hop_bins)
    vmem = pl.BlockSpec(memory_space=pltpu.VMEM)
    hbm = pl.BlockSpec(memory_space=pltpu.HBM)
    operands = (
        echoes,
        matched,
        pulse_phase,
        delays,
        beam_map,
        range_shift,
        phase_base,
        phase_rate,
        tap_offsets,
    )
    extended = hop_bins + 2 * EDGE
    return pl.pallas_call(
        functools.partial(kernel, pulses, beams, span),
        out_shape=jax.ShapeDtypeStruct((parts, beams, blocks * hop_bins), jnp.float32),
        in_specs=[hbm] * len(operands),
        out_specs=vmem,
        scratch_shapes=[
            (pltpu.VMEM if place < 3 else pltpu.SMEM)(operand.shape, operand.dtype)
            for place, operand in enumerate(operands)
        ]
        + [
            pltpu.SemaphoreType.DMA((len(operands),)),
            pltpu.VMEM((2,) + pulse_phase.shape, jnp.float32),
            pltpu.SMEM((2,) + pulse_phase.shape, jnp.float32),
            pltpu.SemaphoreType.DMA,
            pltpu.VMEM((2, 4 * hop_bins, LANES), jnp.bfloat16),
            pltpu.VMEM((pulses, extended, LANES), jnp.float32),
            pltpu.VMEM((beams, extended, LANES), jnp.float32),
            pltpu.VMEM((1, extended, LANES), jnp.float32),
            pltpu.VMEM((2, span, hop_bins + 2 * SHIFT, LANES), jnp.float32),
            pltpu.VMEM((2, 2 * beams, hop_bins, LANES), jnp.float32),
            pltpu.VMEM((levels, span, hop_bins, LANES), jnp.bfloat16),
            pltpu.VMEM((levels, span, hop_bins, LANES), jnp.bfloat16),
            pltpu.VMEM((beams * LANES, hop_bins), jnp.float32),
            pltpu.SemaphoreType.DMA((levels, span)),
            pltpu.SemaphoreType.DMA((levels, span)),
        ],
        compiler_params=pltpu.CompilerParams(
            collective_id=0, has_side_effects=True, vmem_limit_bytes=64946176
        ),
    )(*operands)


def local_any(raw_echoes, *rest):
    pulses, blocks, parts, hop_bins = raw_echoes.shape
    paired = lax.axis_size("pulse") % 2**LEVELS == 0
    if lax.axis_size("rng") == 1 and blocks * parts == LANES and hop_bins == LANES and paired:
        return local_fused(raw_echoes, *rest)
    return local(raw_echoes, *rest)


def solution(mesh):
    in_specs = (
        P(("grp", "pulse"), "rng", None, None),
        P(),
        P(("grp", "pulse"), None),
        P(("grp", "pulse"), None),
        P(),
        P(),
        P(),
        P(),
        P(),
    )
    out_specs = P(None, ("grp", "pulse"), "rng")
    return jax.shard_map(local_any, mesh=mesh, in_specs=in_specs, out_specs=out_specs, check_vma=False)
```

```python
import functools
import math

import jax
import jax.numpy as jnp
from jax import lax
from jax.experimental import pallas as pl
from jax.experimental.pallas import tpu as pltpu
from jax.sharding import PartitionSpec as P

R = 8192
BLOCK = 256
LEVELS = 4
SHIFT = 24
SPREAD = 4


SQRT_HALF = 0.7071067811865476


def shifted(array, axis, by):
    count = lax.axis_size(axis)
    pairs = [(i, i + by) for i in range(count) if 0 <= i + by < count]
    return lax.ppermute(array, axis, pairs)


def padded_2(block, sides, width):
    for axis, dim in sides:
        count = lax.axis_size(axis)
        forward = [(i, i + 1) for i in range(count - 1)]
        backward = [(target, source) for source, target in forward]
        low = lax.ppermute(
            lax.slice_in_dim(block, block.shape[dim] - width, None, axis=dim), axis, forward
        )
        high = lax.ppermute(lax.slice_in_dim(block, 0, width, axis=dim), axis, backward)
        block = jnp.concatenate([low, block, high], axis=dim)
    return block


def from_partner(block, axis, bit):
    count = lax.axis_size(axis)
    route = []
    for low in range(count):
        high = low | 1 << bit
        if high != low and high < count:
            route += [(low, high), (high, low)]
    return lax.ppermute(block, axis, route)


def tables(length):
    counter = jnp.arange(length, dtype=jnp.int32)
    product = counter[:, None] * counter[None, :] % length
    angles = product.astype(jnp.float32) * (2.0 * math.pi / length)
    cosine = jnp.cos(angles)
    sine_part = jnp.sin(angles)
    forward = jnp.concatenate(
        [
            jnp.concatenate([cosine, -sine_part], axis=1),
            jnp.concatenate([sine_part, cosine], axis=1),
        ],
        axis=0,
    )
    inverse = jnp.concatenate(
        [
            jnp.concatenate([cosine, sine_part], axis=1),
            jnp.concatenate([-sine_part, cosine], axis=1),
        ],
        axis=0,
    )
    return (forward, inverse)


def compress(echoes, tail, matched, forward_exact, forward, inverse_kept):
    pulses, blocks, parts, hop_bins = echoes.shape
    length = 2 * hop_bins
    previous = jnp.concatenate([tail[:, None], echoes[:, :-1]], axis=1)
    windows = jnp.concatenate([previous, echoes], axis=3).reshape(pulses * blocks, parts * length)
    taps_padded = jnp.concatenate(
        [matched, jnp.zeros((2, length - hop_bins), jnp.float32)], axis=1
    ).reshape(1, 2 * length)
    response = jnp.dot(taps_padded, forward_exact, precision=lax.Precision.HIGHEST)[0]
    resp_real = response[:length]
    resp_imag = response[length:]
    spectrum = jnp.dot(windows, forward, preferred_element_type=jnp.float32)
    spec_real = spectrum[:, :length]
    spec_imag = spectrum[:, length:]
    filt_real = spec_real * resp_real - spec_imag * resp_imag
    filt_imag = spec_real * resp_imag + spec_imag * resp_real
    shaped = jnp.concatenate([filt_real, filt_imag], axis=1).astype(jnp.bfloat16)
    restored = jnp.dot(shaped, inverse_kept, preferred_element_type=jnp.float32) * (1.0 / length)
    return restored.astype(jnp.bfloat16).reshape(pulses, blocks, parts, hop_bins)


def kept_columns(inverse, length):
    half = length // 2
    return jnp.concatenate([inverse[:, half:length], inverse[:, length + half :]], axis=1)


def inside_mask(first_cell, out_cells):
    global_cells = first_cell + jnp.arange(out_cells, dtype=jnp.int32)
    return ((global_cells >= 0) & (global_cells < R)).astype(jnp.float32)


def row_slices(rows, starts, width):

    def per_pulse(row, start_row):
        return jax.vmap(lambda start: lax.dynamic_slice_in_dim(row, start, width, 1))(start_row)

    return jax.vmap(per_pulse)(rows, starts)


def project(padded, delay_rows, phase_rows, offset_base, out_cells, first_cell):
    pulses = padded.shape[0]
    beam_count = delay_rows.shape[1]
    group_size = math.gcd(pulses, 4)
    block_count = pulses // group_size

    def accumulate(summed, block_index):
        first_row = block_index * group_size
        pulses_block = lax.dynamic_slice_in_dim(padded, first_row, group_size, 0)
        delay_block = lax.dynamic_slice_in_dim(delay_rows, first_row, group_size, 0)
        phase_block = lax.dynamic_slice_in_dim(phase_rows, first_row, group_size, 0)
        starts = delay_block + offset_base
        gathered = row_slices(pulses_block, starts, out_cells).astype(jnp.float32)
        cosine = jnp.cos(phase_block)[:, :, None]
        sine_part = jnp.sin(phase_block)[:, :, None]
        real_part = gathered[:, :, 0] * cosine - gathered[:, :, 1] * sine_part
        imag_part = gathered[:, :, 0] * sine_part + gathered[:, :, 1] * cosine
        return (summed + jnp.stack([jnp.sum(real_part, axis=0), jnp.sum(imag_part, axis=0)]), None)

    summed, unused = lax.scan(
        accumulate,
        jnp.zeros((2, beam_count, out_cells), jnp.float32),
        jnp.arange(block_count, dtype=jnp.int32),
    )
    return summed * inside_mask(first_cell, out_cells) * (1.0 / math.sqrt(pulses))


def tap_weights(tap_values):
    weights = SPREAD + 1.0 - jnp.abs(tap_values).astype(jnp.float32)
    return weights / jnp.sum(weights)


def merge_side(
    source,
    beam_rows,
    offsets,
    phase_zero,
    phase_slope,
    weights,
    tap_values,
    offset_base,
    out_cells,
    first_cell,
):
    picked = jnp.take(source, beam_rows, axis=1)
    span = out_cells + 2 * SPREAD
    starts = offsets + offset_base - SPREAD
    windows = jax.vmap(
        lambda beam_data, start: lax.dynamic_slice_in_dim(beam_data, start, span, 1),
        in_axes=(1, 0),
        out_axes=1,
    )(picked, starts)
    summed = jnp.zeros((2, beam_rows.shape[0], out_cells), jnp.float32)
    for tap_index in range(tap_values.shape[0]):
        tap_start = tap_values[tap_index] + SPREAD
        summed = summed + weights[tap_index] * lax.dynamic_slice_in_dim(
            windows, tap_start, out_cells, 2
        )
    positions = jnp.arange(out_cells, dtype=jnp.int32)
    global_cells = (first_cell + positions).astype(jnp.float32)
    angle_grid = (
        phase_zero[:, None] + 2.0 * math.pi / R * phase_slope[:, None] * global_cells[None, :]
    )
    cosine = jnp.cos(angle_grid)
    sine_part = jnp.sin(angle_grid)
    return jnp.stack(
        [summed[0] * cosine - summed[1] * sine_part, summed[0] * sine_part + summed[1] * cosine]
    )


def pick_sides(table, level_index, side_bit):
    half_rows = lax.dynamic_index_in_dim(table[level_index], side_bit, 0, keepdims=False)
    own_rows = lax.dynamic_index_in_dim(half_rows, side_bit, 0, keepdims=False)
    other_rows = lax.dynamic_index_in_dim(half_rows, 1 - side_bit, 0, keepdims=False)
    return (own_rows, other_rows)


def local(
    raw_echoes,
    matched,
    delays,
    pulse_phase,
    beam_map,
    range_shift,
    phase_base,
    phase_rate,
    tap_offsets,
):
    pulses = raw_echoes.shape[0]
    hop_bins = raw_echoes.shape[3]
    local_cells = raw_echoes.shape[1] * hop_bins
    forward_exact, inverse_exact = tables(BLOCK)
    forward = forward_exact.astype(jnp.bfloat16)
    inverse_kept = kept_columns(inverse_exact.astype(jnp.bfloat16), BLOCK)
    tail = shifted(raw_echoes[:, -1], "rng", 1)
    compressed = compress(raw_echoes, tail, matched, forward_exact, forward, inverse_kept)
    compressed = jnp.transpose(compressed, (0, 2, 1, 3)).reshape(pulses, 2, local_cells)
    first_cell = lax.axis_index("rng") * local_cells
    rim_cells = SHIFT + SPREAD
    margin_cells = LEVELS * rim_cells
    padded = padded_2(compressed, (("rng", 2),), SHIFT + margin_cells)
    polar_image = project(
        padded,
        delays,
        pulse_phase,
        SHIFT,
        local_cells + 2 * margin_cells,
        first_cell - margin_cells,
    )
    pulse_index = lax.axis_index("pulse")
    for level_index in range(LEVELS):
        side_bit = pulse_index // 2**level_index % 2
        own_beams, other_beams = pick_sides(beam_map, level_index, side_bit)
        own_offsets, other_offsets = pick_sides(range_shift, level_index, side_bit)
        own_zero, other_zero = pick_sides(phase_base, level_index, side_bit)
        own_slope, other_slope = pick_sides(phase_rate, level_index, side_bit)
        tap_values = tap_offsets[level_index]
        weights = tap_weights(tap_values)
        received = from_partner(polar_image, "pulse", level_index)
        own_source = polar_image
        out_margin = max(margin_cells - rim_cells * (level_index + 1), 0)
        out_cells = local_cells + 2 * out_margin
        start_cell = first_cell - out_margin
        own_side = merge_side(
            own_source,
            own_beams,
            own_offsets,
            own_zero,
            own_slope,
            weights,
            tap_values,
            rim_cells,
            out_cells,
            start_cell,
        )
        other_side = merge_side(
            received,
            other_beams,
            other_offsets,
            other_zero,
            other_slope,
            weights,
            tap_values,
            rim_cells,
            out_cells,
            start_cell,
        )
        polar_image = (own_side + other_side) * SQRT_HALF * inside_mask(start_cell, out_cells)
    return polar_image


LANES = 128
EDGE = 32


def flip_parts(value, lane):
    return jnp.where(
        lane % 2 == 0, -pltpu.roll(value, LANES - 1, 1), pltpu.roll(value, 1, 1)
    )


def from_previous(value, lane):
    return jnp.where(lane < 2, 0.0, pltpu.roll(value, 2, 1))


def from_next(value, lane):
    return jnp.where(lane >= LANES - 2, 0.0, pltpu.roll(value, LANES - 2, 1))


def store_extended(target, slot, value):
    rows = value.shape[0]
    lane = lax.broadcasted_iota(jnp.int32, (EDGE, LANES), 1)
    target[slot, EDGE : EDGE + rows, :] = value
    target[slot, 0:EDGE, :] = from_previous(value[rows - EDGE :], lane)
    target[slot, EDGE + rows :, :] = from_next(value[:EDGE], lane)


def sin_cos(turns):
    half_turns = jnp.floor(2.0 * turns + 0.5)
    angle = (turns - 0.5 * half_turns) * (2.0 * math.pi)
    sign = 1.0 - 2.0 * (half_turns - 2.0 * jnp.floor(0.5 * half_turns))
    square = angle * angle
    sine = jnp.full_like(angle, -1.0 / math.factorial(11))
    cosine = jnp.full_like(angle, 1.0 / math.factorial(12))
    for power in (9, 7, 5, 3, 1):
        sine = sine * square + (-1.0) ** (power // 2) / math.factorial(power)
    for power in (10, 8, 6, 4, 2, 0):
        cosine = cosine * square + (-1.0) ** (power // 2) / math.factorial(power)
    return sign * angle * sine, sign * cosine


def early_plan(beams, span):
    needs = [0] * span
    for low in (0, beams - span):
        for turn in (0, 2):
            for half in (0, 1):
                for position in range(span):
                    beam = low + (position + turn) % span
                    start = 2 if low else 0
                    for step in (-1, 0, 1):
                        child = min(max(beam // 2 + step + half * (beams // 2), 0), beams - 1)
                        place = (child - half * (beams - span) - start) % span
                        needs[position] = max(needs[position], place + 1)
    plan = []
    for position in range(span):
        need = max(needs[: position + 1])
        if plan and plan[-1][0] == need:
            plan[-1] = (need, position + 1)
        else:
            plan.append((need, position + 1))
    return plan


def kernel(
    pulses,
    beams,
    span,
    *refs,
):
    sources, (out_ref,), held, work = refs[:9], refs[9:10], refs[10:20], refs[20:]
    (
        echo_ref,
        matched_ref,
        phase_ref,
        delay_ref,
        map_ref,
        shift_ref,
        base_ref,
        rate_ref,
        tap_ref,
        load_sem,
    ) = held
    (
    trig_hold,
    trig_ref,
    trig_sem,
    taps_hold,
    pulse_ext,
    image,
    other,
    filt,
    table,
    outgoing,
    incoming,
    turned,
    send_sem,
    recv_sem,
    ) = work
    loads = [
        pltpu.make_async_copy(source, target, load_sem.at[place])
        for place, (source, target) in enumerate(zip(sources, held))
    ]
    for place in (2, 1, 0, 3, 4, 5, 6, 7, 8):
        loads[place].start()
    levels = tap_ref.shape[0]
    tap_count = tap_ref.shape[1]
    rows = echo_ref.shape[1]
    me = lax.axis_index("pulse")
    partners = []
    bits = []
    for level in range(levels):
        bit = me // 2**level % 2
        bits.append(bit)
        partners.append(me + (1 - 2 * bit) * 2**level)

    turns = [2 * (1 - bits[level + 1]) for level in range(levels - 1)] + [0]

    barrier = pltpu.get_barrier_semaphore()
    for partner in partners:
        pl.semaphore_signal(
            barrier, inc=1, device_id={"pulse": partner}, device_id_type=pl.DeviceIdType.MESH
        )

    lane = lax.broadcasted_iota(jnp.int32, (rows, LANES), 1)
    row = lax.broadcasted_iota(jnp.int32, (rows, LANES), 0)

    loads[2].wait()
    sine, cosine = sin_cos(phase_ref[...] * (0.5 / math.pi))
    trig_hold[0] = cosine * (1.0 / math.sqrt(pulses))
    trig_hold[1] = sine * (1.0 / math.sqrt(pulses))
    to_scalars = pltpu.make_async_copy(trig_hold, trig_ref, trig_sem)
    to_scalars.start()
    loads[1].wait()

    for part in range(2):
        spread_taps = jnp.broadcast_to(matched_ref[part : part + 1, :], (rows, LANES))
        circulant = jnp.transpose(pltpu.roll(spread_taps, 0, 1, stride=1, stride_axis=0))
        for side in range(2):
            kept = jnp.where((row >= lane) == (side == 0), circulant, 0.0)
            high = kept.astype(jnp.bfloat16)
            low = (kept - high.astype(jnp.float32)).astype(jnp.bfloat16)
            place = (part * 2 + side) * rows
            taps_hold[0, place : place + rows, :] = high
            taps_hold[1, place : place + rows, :] = low

    def compress_pulse(pulse, carry):
        first = pl.multiple_of(pulse * LANES, LANES)
        data = echo_ref[pl.ds(first, LANES), :]

        def times(part, side):
            place = (part * 2 + side) * rows
            dims = (((1,), (1,)), ((), ()))
            return lax.dot_general(
                taps_hold[0, place : place + rows, :], data, dims, preferred_element_type=jnp.float32
            ) + lax.dot_general(
                taps_hold[1, place : place + rows, :], data, dims, preferred_element_type=jnp.float32
            )

        real_taps = times(0, 0) + from_previous(times(0, 1), lane)
        imag_taps = times(1, 0) + from_previous(times(1, 1), lane)
        store_extended(pulse_ext, pulse, real_taps + flip_parts(imag_taps, lane))
        return carry

    loads[0].wait()
    lax.fori_loop(0, pulses, compress_pulse, 0)
    for load in loads[3:]:
        load.wait()
    to_scalars.wait()

    def beam_at(level, position):
        first = (1 - bits[level]) * (beams - span)
        early = first + lax.rem(position + turns[level], span)
        late = bits[level] * span + position - span
        return early, late

    def transfer(level, position):
        return pltpu.make_async_remote_copy(
            src_ref=outgoing.at[level, position],
            dst_ref=incoming.at[level, position],
            send_sem=send_sem.at[level, position],
            recv_sem=recv_sem.at[level, position],
            device_id={"pulse": partners[level]},
            device_id_type=pl.DeviceIdType.MESH,
        )

    def project_beam(beam):
        cos_sum = jnp.zeros((rows, LANES), jnp.float32)
        sin_sum = jnp.zeros((rows, LANES), jnp.float32)
        for pulse in range(pulses):
            slab = pulse_ext[pulse, pl.ds(EDGE + delay_ref[pulse, beam], rows), :]
            cos_sum += trig_ref[0, pulse, beam] * slab
            sin_sum += trig_ref[1, pulse, beam] * slab
        return cos_sum + flip_parts(sin_sum, lane)

    def produce(level, make, low, high):
        def step(position, carry):
            early, late = beam_at(level, position)
            beam = early if high <= span else late
            value = make(beam)
            if high <= span:
                outgoing[level, position] = value.astype(jnp.bfloat16)
                transfer(level, position).start()
            store_extended(image, beam, value)
            return carry

        lax.fori_loop(low, high, step, 0, unroll=min(high - low, 3))

    def put_group(group):
        def put_block(block, carry):
            column = pl.multiple_of(block * rows, rows)
            for part in range(2):
                start = group * 8 * LANES + 2 * block + part
                out_ref[part, group * 8 : group * 8 + 8, pl.ds(column, rows)] = turned[
                    pl.ds(start, 8, stride=LANES), :
                ]
            return carry

        lax.fori_loop(0, LANES // 2, put_block, 0, unroll=4)

    pl.semaphore_wait(barrier, levels)
    produce(0, project_beam, 0, span)
    produce(0, project_beam, span, beams)

    small_lane = lax.broadcasted_iota(jnp.int32, (8, LANES), 1)
    small_row = lax.broadcasted_iota(jnp.int32, (8, LANES), 0)
    cells = (small_lane // 2 * rows + small_row).astype(jnp.float32)
    filt_rows = filt.shape[2]
    for level in range(levels):
        bit = bits[level]
        own_first = bit * (beams - span)

        raw_weights = [
            jnp.full(
                (8, LANES), SPREAD + 1 - jnp.abs(tap_ref[level, tap]), jnp.int32
            ).astype(jnp.float32)
            for tap in range(tap_count)
        ]
        total = raw_weights[0]
        for weight in raw_weights[1:]:
            total = total + weight
        weights = [
            jnp.tile(weight * SQRT_HALF / total, (filt_rows // 8, 1)) for weight in raw_weights
        ]

        def fill_one(side, beam, level=level, bit=bit):
            index = side * beams + beam
            zero = base_ref[level, bit, side, beam] * (0.5 / math.pi)
            slope = rate_ref[level, bit, side, beam] * (1.0 / R)
            sine, cosine = sin_cos(zero + slope * cells)
            step_sin, step_cos = sin_cos(jnp.full((8, LANES), slope * 8.0, jnp.float32))
            stack = [(cosine, sine)]
            while len(stack) * 8 < rows:
                stack = stack + [
                    (c * step_cos - s * step_sin, s * step_cos + c * step_sin) for c, s in stack
                ]
                step_cos, step_sin = (
                    step_cos * step_cos - step_sin * step_sin,
                    2.0 * step_cos * step_sin,
                )
            for place, (c, s) in enumerate(stack):
                table[0, index, place * 8 : place * 8 + 8, :] = c
                table[1, index, place * 8 : place * 8 + 8, :] = s

        def fill_table(beam, carry, fill_one=fill_one):
            fill_one(0, beam)
            fill_one(1, beam)
            return carry

        def filter_rows(source, slot, level=level, weights=weights):
            summed = None
            for tap in range(tap_count):
                start = EDGE - SHIFT + tap_ref[level, tap]
                term = weights[tap] * source[slot, pl.ds(start, filt_rows), :]
                summed = term if summed is None else summed + term
            return summed

        def filter_own(index, carry, own_first=own_first, filter_rows=filter_rows):
            filt[0, index] = filter_rows(image, own_first + index)
            return carry

        def filter_other(position, carry, level=level, filter_rows=filter_rows):
            transfer(level, position).wait_recv()
            place = lax.rem(position + turns[level], span)
            store_extended(other, 0, incoming[level, position].astype(jnp.float32))
            filt[1, place] = filter_rows(other, 0)
            return carry

        def slab_of(which, side, beam, level=level, bit=bit, own_first=own_first):
            source = jnp.clip(map_ref[level, bit, side, beam] - own_first, 0, span - 1)
            start = SHIFT + shift_ref[level, bit, side, beam]
            return filt[which, source, pl.ds(start, rows), :]

        def merge(beam, bit=bit, slab_of=slab_of):
            own_slab, own_index = slab_of(0, bit, beam), bit * beams + beam
            other_slab, other_index = slab_of(1, 1 - bit, beam), (1 - bit) * beams + beam
            cos_sum = table[0, own_index] * own_slab + table[0, other_index] * other_slab
            sin_sum = table[1, own_index] * own_slab + table[1, other_index] * other_slab
            return cos_sum + flip_parts(sin_sum, lane)

        def finish(beam, carry, merge=merge):
            first = pl.multiple_of(beam * LANES, LANES)
            turned[pl.ds(first, LANES), :] = jnp.transpose(merge(beam))
            return carry

        lax.fori_loop(0, span, filter_own, 0, unroll=3)
        lax.fori_loop(0, beams, fill_table, 0, unroll=2)
        arrived = 0
        if level + 1 < levels:
            made = 0
            for count, until in early_plan(beams, span):
                lax.fori_loop(arrived, count, filter_other, 0)
                produce(level + 1, merge, made, until)
                arrived, made = count, until
            lax.fori_loop(arrived, span, filter_other, 0)
            produce(level + 1, merge, span, beams)
        else:
            lax.fori_loop(0, 2, filter_other, 0)

            def child_then_pair(position, carry, filter_other=filter_other, finish=finish):
                filter_other(position, 0)
                return lax.fori_loop(2 * position - 4, 2 * position - 2, finish, carry)

            done = 2
            for group in range(beams // 8):
                until = min(4 * group + 6, span)
                lax.fori_loop(done, until, child_then_pair, 0)
                lax.fori_loop(2 * until - 4, 8 * group + 8, finish, 0)
                put_group(group)
                done = until

    def drain(position, carry):
        for level in range(levels):
            transfer(level, position).wait_send()
        return carry

    lax.fori_loop(0, span, drain, 0)


def local_fused(
    raw_echoes,
    matched,
    delays,
    pulse_phase,
    beam_map,
    range_shift,
    phase_base,
    phase_rate,
    tap_offsets,
):
    pulses, blocks, parts, hop_bins = raw_echoes.shape
    beams = delays.shape[1]
    levels = tap_offsets.shape[0]
    span = beams // 2 + 1
    echoes = raw_echoes.reshape(pulses * blocks * parts, hop_bins)
    vmem = pl.BlockSpec(memory_space=pltpu.VMEM)
    hbm = pl.BlockSpec(memory_space=pltpu.HBM)
    operands = (
        echoes,
        matched,
        pulse_phase,
        delays,
        beam_map,
        range_shift,
        phase_base,
        phase_rate,
        tap_offsets,
    )
    extended = hop_bins + 2 * EDGE
    return pl.pallas_call(
        functools.partial(kernel, pulses, beams, span),
        out_shape=jax.ShapeDtypeStruct((parts, beams, blocks * hop_bins), jnp.float32),
        in_specs=[hbm] * len(operands),
        out_specs=vmem,
        scratch_shapes=[
            (pltpu.VMEM if place < 3 else pltpu.SMEM)(operand.shape, operand.dtype)
            for place, operand in enumerate(operands)
        ]
        + [
            pltpu.SemaphoreType.DMA((len(operands),)),
            pltpu.VMEM((2,) + pulse_phase.shape, jnp.float32),
            pltpu.SMEM((2,) + pulse_phase.shape, jnp.float32),
            pltpu.SemaphoreType.DMA,
            pltpu.VMEM((2, 4 * hop_bins, LANES), jnp.bfloat16),
            pltpu.VMEM((pulses, extended, LANES), jnp.float32),
            pltpu.VMEM((beams, extended, LANES), jnp.float32),
            pltpu.VMEM((1, extended, LANES), jnp.float32),
            pltpu.VMEM((2, span, hop_bins + 2 * SHIFT, LANES), jnp.float32),
            pltpu.VMEM((2, 2 * beams, hop_bins, LANES), jnp.float32),
            pltpu.VMEM((levels, span, hop_bins, LANES), jnp.bfloat16),
            pltpu.VMEM((levels, span, hop_bins, LANES), jnp.bfloat16),
            pltpu.VMEM((beams * LANES, hop_bins), jnp.float32),
            pltpu.SemaphoreType.DMA((levels, span)),
            pltpu.SemaphoreType.DMA((levels, span)),
        ],
        compiler_params=pltpu.CompilerParams(
            collective_id=0, has_side_effects=True, vmem_limit_bytes=48 * 2**20
        ),
    )(*[pltpu.with_memory_space_constraint(operand, pltpu.HBM) for operand in operands])


def local_any(raw_echoes, *rest):
    pulses, blocks, parts, hop_bins = raw_echoes.shape
    paired = lax.axis_size("pulse") % 2**LEVELS == 0
    if lax.axis_size("rng") == 1 and blocks * parts == LANES and hop_bins == LANES and paired:
        return local_fused(raw_echoes, *rest)
    return local(raw_echoes, *rest)


def solution(mesh):
    in_specs = (
        P(("grp", "pulse"), "rng", None, None),
        P(),
        P(("grp", "pulse"), None),
        P(("grp", "pulse"), None),
        P(),
        P(),
        P(),
        P(),
        P(),
    )
    out_specs = P(None, ("grp", "pulse"), "rng")
    return jax.shard_map(local_any, mesh=mesh, in_specs=in_specs, out_specs=out_specs, check_vma=False)
```

```python
import functools
import math

import jax
import jax.numpy as jnp
from jax import lax
from jax.experimental import pallas as pl
from jax.experimental.pallas import tpu as pltpu
from jax.sharding import PartitionSpec as P

R = 8192
BLOCK = 256
LEVELS = 4
SHIFT = 24
SPREAD = 4


SQRT_HALF = 0.7071067811865476


def shifted(array, axis, by):
    count = lax.axis_size(axis)
    pairs = [(i, i + by) for i in range(count) if 0 <= i + by < count]
    return lax.ppermute(array, axis, pairs)


def padded_2(block, sides, width):
    for axis, dim in sides:
        count = lax.axis_size(axis)
        forward = [(i, i + 1) for i in range(count - 1)]
        backward = [(target, source) for source, target in forward]
        low = lax.ppermute(
            lax.slice_in_dim(block, block.shape[dim] - width, None, axis=dim), axis, forward
        )
        high = lax.ppermute(lax.slice_in_dim(block, 0, width, axis=dim), axis, backward)
        block = jnp.concatenate([low, block, high], axis=dim)
    return block


def from_partner(block, axis, bit):
    count = lax.axis_size(axis)
    route = []
    for low in range(count):
        high = low | 1 << bit
        if high != low and high < count:
            route += [(low, high), (high, low)]
    return lax.ppermute(block, axis, route)


def tables(length):
    counter = jnp.arange(length, dtype=jnp.int32)
    product = counter[:, None] * counter[None, :] % length
    angles = product.astype(jnp.float32) * (2.0 * math.pi / length)
    cosine = jnp.cos(angles)
    sine_part = jnp.sin(angles)
    forward = jnp.concatenate(
        [
            jnp.concatenate([cosine, -sine_part], axis=1),
            jnp.concatenate([sine_part, cosine], axis=1),
        ],
        axis=0,
    )
    inverse = jnp.concatenate(
        [
            jnp.concatenate([cosine, sine_part], axis=1),
            jnp.concatenate([-sine_part, cosine], axis=1),
        ],
        axis=0,
    )
    return (forward, inverse)


def compress(echoes, tail, matched, forward_exact, forward, inverse_kept):
    pulses, blocks, parts, hop_bins = echoes.shape
    length = 2 * hop_bins
    previous = jnp.concatenate([tail[:, None], echoes[:, :-1]], axis=1)
    windows = jnp.concatenate([previous, echoes], axis=3).reshape(pulses * blocks, parts * length)
    taps_padded = jnp.concatenate(
        [matched, jnp.zeros((2, length - hop_bins), jnp.float32)], axis=1
    ).reshape(1, 2 * length)
    response = jnp.dot(taps_padded, forward_exact, precision=lax.Precision.HIGHEST)[0]
    resp_real = response[:length]
    resp_imag = response[length:]
    spectrum = jnp.dot(windows, forward, preferred_element_type=jnp.float32)
    spec_real = spectrum[:, :length]
    spec_imag = spectrum[:, length:]
    filt_real = spec_real * resp_real - spec_imag * resp_imag
    filt_imag = spec_real * resp_imag + spec_imag * resp_real
    shaped = jnp.concatenate([filt_real, filt_imag], axis=1).astype(jnp.bfloat16)
    restored = jnp.dot(shaped, inverse_kept, preferred_element_type=jnp.float32) * (1.0 / length)
    return restored.astype(jnp.bfloat16).reshape(pulses, blocks, parts, hop_bins)


def kept_columns(inverse, length):
    half = length // 2
    return jnp.concatenate([inverse[:, half:length], inverse[:, length + half :]], axis=1)


def inside_mask(first_cell, out_cells):
    global_cells = first_cell + jnp.arange(out_cells, dtype=jnp.int32)
    return ((global_cells >= 0) & (global_cells < R)).astype(jnp.float32)


def row_slices(rows, starts, width):

    def per_pulse(row, start_row):
        return jax.vmap(lambda start: lax.dynamic_slice_in_dim(row, start, width, 1))(start_row)

    return jax.vmap(per_pulse)(rows, starts)


def project(padded, delay_rows, phase_rows, offset_base, out_cells, first_cell):
    pulses = padded.shape[0]
    beam_count = delay_rows.shape[1]
    group_size = math.gcd(pulses, 4)
    block_count = pulses // group_size

    def accumulate(summed, block_index):
        first_row = block_index * group_size
        pulses_block = lax.dynamic_slice_in_dim(padded, first_row, group_size, 0)
        delay_block = lax.dynamic_slice_in_dim(delay_rows, first_row, group_size, 0)
        phase_block = lax.dynamic_slice_in_dim(phase_rows, first_row, group_size, 0)
        starts = delay_block + offset_base
        gathered = row_slices(pulses_block, starts, out_cells).astype(jnp.float32)
        cosine = jnp.cos(phase_block)[:, :, None]
        sine_part = jnp.sin(phase_block)[:, :, None]
        real_part = gathered[:, :, 0] * cosine - gathered[:, :, 1] * sine_part
        imag_part = gathered[:, :, 0] * sine_part + gathered[:, :, 1] * cosine
        return (summed + jnp.stack([jnp.sum(real_part, axis=0), jnp.sum(imag_part, axis=0)]), None)

    summed, unused = lax.scan(
        accumulate,
        jnp.zeros((2, beam_count, out_cells), jnp.float32),
        jnp.arange(block_count, dtype=jnp.int32),
    )
    return summed * inside_mask(first_cell, out_cells) * (1.0 / math.sqrt(pulses))


def tap_weights(tap_values):
    weights = SPREAD + 1.0 - jnp.abs(tap_values).astype(jnp.float32)
    return weights / jnp.sum(weights)


def merge_side(
    source,
    beam_rows,
    offsets,
    phase_zero,
    phase_slope,
    weights,
    tap_values,
    offset_base,
    out_cells,
    first_cell,
):
    picked = jnp.take(source, beam_rows, axis=1)
    span = out_cells + 2 * SPREAD
    starts = offsets + offset_base - SPREAD
    windows = jax.vmap(
        lambda beam_data, start: lax.dynamic_slice_in_dim(beam_data, start, span, 1),
        in_axes=(1, 0),
        out_axes=1,
    )(picked, starts)
    summed = jnp.zeros((2, beam_rows.shape[0], out_cells), jnp.float32)
    for tap_index in range(tap_values.shape[0]):
        tap_start = tap_values[tap_index] + SPREAD
        summed = summed + weights[tap_index] * lax.dynamic_slice_in_dim(
            windows, tap_start, out_cells, 2
        )
    positions = jnp.arange(out_cells, dtype=jnp.int32)
    global_cells = (first_cell + positions).astype(jnp.float32)
    angle_grid = (
        phase_zero[:, None] + 2.0 * math.pi / R * phase_slope[:, None] * global_cells[None, :]
    )
    cosine = jnp.cos(angle_grid)
    sine_part = jnp.sin(angle_grid)
    return jnp.stack(
        [summed[0] * cosine - summed[1] * sine_part, summed[0] * sine_part + summed[1] * cosine]
    )


def pick_sides(table, level_index, side_bit):
    half_rows = lax.dynamic_index_in_dim(table[level_index], side_bit, 0, keepdims=False)
    own_rows = lax.dynamic_index_in_dim(half_rows, side_bit, 0, keepdims=False)
    other_rows = lax.dynamic_index_in_dim(half_rows, 1 - side_bit, 0, keepdims=False)
    return (own_rows, other_rows)


def local(
    raw_echoes,
    matched,
    delays,
    pulse_phase,
    beam_map,
    range_shift,
    phase_base,
    phase_rate,
    tap_offsets,
):
    pulses = raw_echoes.shape[0]
    hop_bins = raw_echoes.shape[3]
    local_cells = raw_echoes.shape[1] * hop_bins
    forward_exact, inverse_exact = tables(BLOCK)
    forward = forward_exact.astype(jnp.bfloat16)
    inverse_kept = kept_columns(inverse_exact.astype(jnp.bfloat16), BLOCK)
    tail = shifted(raw_echoes[:, -1], "rng", 1)
    compressed = compress(raw_echoes, tail, matched, forward_exact, forward, inverse_kept)
    compressed = jnp.transpose(compressed, (0, 2, 1, 3)).reshape(pulses, 2, local_cells)
    first_cell = lax.axis_index("rng") * local_cells
    rim_cells = SHIFT + SPREAD
    margin_cells = LEVELS * rim_cells
    padded = padded_2(compressed, (("rng", 2),), SHIFT + margin_cells)
    polar_image = project(
        padded,
        delays,
        pulse_phase,
        SHIFT,
        local_cells + 2 * margin_cells,
        first_cell - margin_cells,
    )
    pulse_index = lax.axis_index("pulse")
    for level_index in range(LEVELS):
        side_bit = pulse_index // 2**level_index % 2
        own_beams, other_beams = pick_sides(beam_map, level_index, side_bit)
        own_offsets, other_offsets = pick_sides(range_shift, level_index, side_bit)
        own_zero, other_zero = pick_sides(phase_base, level_index, side_bit)
        own_slope, other_slope = pick_sides(phase_rate, level_index, side_bit)
        tap_values = tap_offsets[level_index]
        weights = tap_weights(tap_values)
        received = from_partner(polar_image, "pulse", level_index)
        own_source = polar_image
        out_margin = max(margin_cells - rim_cells * (level_index + 1), 0)
        out_cells = local_cells + 2 * out_margin
        start_cell = first_cell - out_margin
        own_side = merge_side(
            own_source,
            own_beams,
            own_offsets,
            own_zero,
            own_slope,
            weights,
            tap_values,
            rim_cells,
            out_cells,
            start_cell,
        )
        other_side = merge_side(
            received,
            other_beams,
            other_offsets,
            other_zero,
            other_slope,
            weights,
            tap_values,
            rim_cells,
            out_cells,
            start_cell,
        )
        polar_image = (own_side + other_side) * SQRT_HALF * inside_mask(start_cell, out_cells)
    return polar_image


LANES = 128
EDGE = 32


def flip_parts(value, lane):
    return jnp.where(
        lane % 2 == 0, -pltpu.roll(value, LANES - 1, 1), pltpu.roll(value, 1, 1)
    )


def from_previous(value, lane):
    return jnp.where(lane < 2, 0.0, pltpu.roll(value, 2, 1))


def from_next(value, lane):
    return jnp.where(lane >= LANES - 2, 0.0, pltpu.roll(value, LANES - 2, 1))


def store_extended(target, slot, value):
    rows = value.shape[0]
    lane = lax.broadcasted_iota(jnp.int32, (EDGE, LANES), 1)
    target[slot, EDGE : EDGE + rows, :] = value
    target[slot, 0:EDGE, :] = from_previous(value[rows - EDGE :], lane)
    target[slot, EDGE + rows :, :] = from_next(value[:EDGE], lane)


def sin_cos(turns):
    half_turns = jnp.floor(2.0 * turns + 0.5)
    angle = (turns - 0.5 * half_turns) * (2.0 * math.pi)
    sign = 1.0 - 2.0 * (half_turns - 2.0 * jnp.floor(0.5 * half_turns))
    square = angle * angle
    sine = jnp.full_like(angle, -1.0 / math.factorial(11))
    cosine = jnp.full_like(angle, 1.0 / math.factorial(12))
    for power in (9, 7, 5, 3, 1):
        sine = sine * square + (-1.0) ** (power // 2) / math.factorial(power)
    for power in (10, 8, 6, 4, 2, 0):
        cosine = cosine * square + (-1.0) ** (power // 2) / math.factorial(power)
    return sign * angle * sine, sign * cosine


def early_plan(beams, span):
    needs = [0] * span
    for low in (0, beams - span):
        for turn in (0, 2):
            for half in (0, 1):
                for position in range(span):
                    beam = low + (position + turn) % span
                    start = 2 if low else 0
                    for step in (-1, 0, 1):
                        child = min(max(beam // 2 + step + half * (beams // 2), 0), beams - 1)
                        place = (child - half * (beams - span) - start) % span
                        needs[position] = max(needs[position], place + 1)
    plan = []
    for position in range(span):
        need = max(needs[: position + 1])
        if plan and plan[-1][0] == need:
            plan[-1] = (need, position + 1)
        else:
            plan.append((need, position + 1))
    return plan


def kernel(
    pulses,
    beams,
    span,
    *refs,
):
    sources, (out_ref,), held, work = refs[:9], refs[9:10], refs[10:20], refs[20:]
    (
        echo_ref,
        matched_ref,
        phase_ref,
        delay_ref,
        map_ref,
        shift_ref,
        base_ref,
        rate_ref,
        tap_ref,
        load_sem,
    ) = held
    (
    trig_hold,
    trig_ref,
    trig_sem,
    taps_hold,
    pulse_ext,
    image,
    other,
    filt,
    table,
    outgoing,
    incoming,
    turned,
    send_sem,
    recv_sem,
    ) = work
    loads = [
        pltpu.make_async_copy(source, target, load_sem.at[place])
        for place, (source, target) in enumerate(zip(sources, held))
    ]
    for place in (2, 1, 0, 3, 4, 5, 6, 7, 8):
        loads[place].start()
    levels = tap_ref.shape[0]
    tap_count = tap_ref.shape[1]
    rows = echo_ref.shape[1]
    me = lax.axis_index("pulse")
    partners = []
    bits = []
    for level in range(levels):
        bit = me // 2**level % 2
        bits.append(bit)
        partners.append(me + (1 - 2 * bit) * 2**level)

    turns = [2 * (1 - bits[level + 1]) for level in range(levels - 1)] + [0]

    barrier = pltpu.get_barrier_semaphore()
    for partner in partners:
        pl.semaphore_signal(
            barrier, inc=1, device_id={"pulse": partner}, device_id_type=pl.DeviceIdType.MESH
        )

    lane = lax.broadcasted_iota(jnp.int32, (rows, LANES), 1)
    row = lax.broadcasted_iota(jnp.int32, (rows, LANES), 0)

    loads[2].wait()
    sine, cosine = sin_cos(phase_ref[...] * (0.5 / math.pi))
    trig_hold[0] = cosine * (1.0 / math.sqrt(pulses))
    trig_hold[1] = sine * (1.0 / math.sqrt(pulses))
    to_scalars = pltpu.make_async_copy(trig_hold, trig_ref, trig_sem)
    to_scalars.start()
    loads[1].wait()

    for part in range(2):
        spread_taps = jnp.broadcast_to(matched_ref[part : part + 1, :], (rows, LANES))
        circulant = jnp.transpose(pltpu.roll(spread_taps, 0, 1, stride=1, stride_axis=0))
        for side in range(2):
            kept = jnp.where((row >= lane) == (side == 0), circulant, 0.0)
            high = kept.astype(jnp.bfloat16)
            low = (kept - high.astype(jnp.float32)).astype(jnp.bfloat16)
            place = (part * 2 + side) * rows
            taps_hold[0, place : place + rows, :] = high
            taps_hold[1, place : place + rows, :] = low

    def compress_pulse(pulse, carry):
        first = pl.multiple_of(pulse * LANES, LANES)
        data = echo_ref[pl.ds(first, LANES), :]

        def times(part, side):
            place = (part * 2 + side) * rows
            dims = (((1,), (1,)), ((), ()))
            return lax.dot_general(
                taps_hold[0, place : place + rows, :], data, dims, preferred_element_type=jnp.float32
            ) + lax.dot_general(
                taps_hold[1, place : place + rows, :], data, dims, preferred_element_type=jnp.float32
            )

        real_taps = times(0, 0) + from_previous(times(0, 1), lane)
        imag_taps = times(1, 0) + from_previous(times(1, 1), lane)
        store_extended(pulse_ext, pulse, real_taps + flip_parts(imag_taps, lane))
        return carry

    loads[0].wait()
    lax.fori_loop(0, pulses, compress_pulse, 0, unroll=2)
    for load in loads[3:]:
        load.wait()
    to_scalars.wait()

    def beam_at(level, position):
        first = (1 - bits[level]) * (beams - span)
        early = first + lax.rem(position + turns[level], span)
        late = bits[level] * span + position - span
        return early, late

    def transfer(level, position):
        return pltpu.make_async_remote_copy(
            src_ref=outgoing.at[level, position],
            dst_ref=incoming.at[level, position],
            send_sem=send_sem.at[level, position],
            recv_sem=recv_sem.at[level, position],
            device_id={"pulse": partners[level]},
            device_id_type=pl.DeviceIdType.MESH,
        )

    def project_beam(beam):
        cos_sum = jnp.zeros((rows, LANES), jnp.float32)
        sin_sum = jnp.zeros((rows, LANES), jnp.float32)
        for pulse in range(pulses):
            slab = pulse_ext[pulse, pl.ds(EDGE + delay_ref[pulse, beam], rows), :]
            cos_sum += trig_ref[0, pulse, beam] * slab
            sin_sum += trig_ref[1, pulse, beam] * slab
        return cos_sum + flip_parts(sin_sum, lane)

    def produce(level, make, low, high):
        def step(position, carry):
            early, late = beam_at(level, position)
            beam = early if high <= span else late
            value = make(beam)
            if high <= span:
                outgoing[level, position] = value.astype(jnp.bfloat16)
                transfer(level, position).start()
            store_extended(image, beam, value)
            return carry

        lax.fori_loop(low, high, step, 0, unroll=True)

    def put_group(group):
        def put_block(block, carry):
            column = pl.multiple_of(block * rows, rows)
            for part in range(2):
                start = group * 8 * LANES + 2 * block + part
                out_ref[part, group * 8 : group * 8 + 8, pl.ds(column, rows)] = turned[
                    pl.ds(start, 8, stride=LANES), :
                ]
            return carry

        lax.fori_loop(0, LANES // 2, put_block, 0, unroll=4)

    pl.semaphore_wait(barrier, levels)
    produce(0, project_beam, 0, span)
    produce(0, project_beam, span, beams)

    small_lane = lax.broadcasted_iota(jnp.int32, (8, LANES), 1)
    small_row = lax.broadcasted_iota(jnp.int32, (8, LANES), 0)
    cells = (small_lane // 2 * rows + small_row).astype(jnp.float32)
    filt_rows = filt.shape[2]
    for level in range(levels):
        bit = bits[level]
        own_first = bit * (beams - span)

        raw_weights = [
            jnp.full(
                (8, LANES), SPREAD + 1 - jnp.abs(tap_ref[level, tap]), jnp.int32
            ).astype(jnp.float32)
            for tap in range(tap_count)
        ]
        total = raw_weights[0]
        for weight in raw_weights[1:]:
            total = total + weight
        weights = [
            jnp.tile(weight * SQRT_HALF / total, (filt_rows // 8, 1)) for weight in raw_weights
        ]

        def fill_one(side, beam, level=level, bit=bit):
            index = side * beams + beam
            zero = base_ref[level, bit, side, beam] * (0.5 / math.pi)
            slope = rate_ref[level, bit, side, beam] * (1.0 / R)
            sine, cosine = sin_cos(zero + slope * cells)
            step_sin, step_cos = sin_cos(jnp.full((8, LANES), slope * 8.0, jnp.float32))
            stack = [(cosine, sine)]
            while len(stack) * 8 < rows:
                stack = stack + [
                    (c * step_cos - s * step_sin, s * step_cos + c * step_sin) for c, s in stack
                ]
                step_cos, step_sin = (
                    step_cos * step_cos - step_sin * step_sin,
                    2.0 * step_cos * step_sin,
                )
            for place, (c, s) in enumerate(stack):
                table[0, index, place * 8 : place * 8 + 8, :] = c
                table[1, index, place * 8 : place * 8 + 8, :] = s

        def fill_table(beam, carry, fill_one=fill_one):
            fill_one(0, beam)
            fill_one(1, beam)
            return carry

        def filter_rows(source, slot, level=level, weights=weights):
            summed = None
            for tap in range(tap_count):
                start = EDGE - SHIFT + tap_ref[level, tap]
                term = weights[tap] * source[slot, pl.ds(start, filt_rows), :]
                summed = term if summed is None else summed + term
            return summed

        def filter_own(index, carry, own_first=own_first, filter_rows=filter_rows):
            filt[0, index] = filter_rows(image, own_first + index)
            return carry

        def filter_other(position, carry, level=level, filter_rows=filter_rows):
            transfer(level, position).wait_recv()
            place = lax.rem(position + turns[level], span)
            store_extended(other, 0, incoming[level, position].astype(jnp.float32))
            filt[1, place] = filter_rows(other, 0)
            return carry

        def slab_of(which, side, beam, level=level, bit=bit, own_first=own_first):
            source = jnp.clip(map_ref[level, bit, side, beam] - own_first, 0, span - 1)
            start = SHIFT + shift_ref[level, bit, side, beam]
            return filt[which, source, pl.ds(start, rows), :]

        def merge(beam, bit=bit, slab_of=slab_of):
            own_slab, own_index = slab_of(0, bit, beam), bit * beams + beam
            other_slab, other_index = slab_of(1, 1 - bit, beam), (1 - bit) * beams + beam
            cos_sum = table[0, own_index] * own_slab + table[0, other_index] * other_slab
            sin_sum = table[1, own_index] * own_slab + table[1, other_index] * other_slab
            return cos_sum + flip_parts(sin_sum, lane)

        def finish(beam, carry, merge=merge):
            first = pl.multiple_of(beam * LANES, LANES)
            turned[pl.ds(first, LANES), :] = jnp.transpose(merge(beam))
            return carry

        lax.fori_loop(0, span, filter_own, 0, unroll=True)
        lax.fori_loop(0, beams, fill_table, 0, unroll=4)
        arrived = 0
        if level + 1 < levels:
            made = 0
            for count, until in early_plan(beams, span):
                lax.fori_loop(arrived, count, filter_other, 0, unroll=True)
                produce(level + 1, merge, made, until)
                arrived, made = count, until
            lax.fori_loop(arrived, span, filter_other, 0)
            produce(level + 1, merge, span, beams)
        else:
            lax.fori_loop(0, 2, filter_other, 0)

            def child_then_pair(position, carry, filter_other=filter_other, finish=finish):
                filter_other(position, 0)
                return finish(2 * position - 3, finish(2 * position - 4, carry))

            done = 2
            for group in range(beams // 8):
                until = min(4 * group + 6, span)
                lax.fori_loop(done, until, child_then_pair, 0)
                lax.fori_loop(2 * until - 4, 8 * group + 8, finish, 0, unroll=True)
                put_group(group)
                done = until

    def drain(position, carry):
        for level in range(levels):
            transfer(level, position).wait_send()
        return carry

    lax.fori_loop(0, span, drain, 0)


def local_fused(
    raw_echoes,
    matched,
    delays,
    pulse_phase,
    beam_map,
    range_shift,
    phase_base,
    phase_rate,
    tap_offsets,
):
    pulses, blocks, parts, hop_bins = raw_echoes.shape
    beams = delays.shape[1]
    levels = tap_offsets.shape[0]
    span = beams // 2 + 1
    echoes = raw_echoes.reshape(pulses * blocks * parts, hop_bins)
    vmem = pl.BlockSpec(memory_space=pltpu.VMEM)
    hbm = pl.BlockSpec(memory_space=pltpu.HBM)
    operands = (
        echoes,
        matched,
        pulse_phase,
        delays,
        beam_map,
        range_shift,
        phase_base,
        phase_rate,
        tap_offsets,
    )
    extended = hop_bins + 2 * EDGE
    return pl.pallas_call(
        functools.partial(kernel, pulses, beams, span),
        out_shape=jax.ShapeDtypeStruct((parts, beams, blocks * hop_bins), jnp.float32),
        in_specs=[hbm] * len(operands),
        out_specs=vmem,
        scratch_shapes=[
            (pltpu.VMEM if place < 3 else pltpu.SMEM)(operand.shape, operand.dtype)
            for place, operand in enumerate(operands)
        ]
        + [
            pltpu.SemaphoreType.DMA((len(operands),)),
            pltpu.VMEM((2,) + pulse_phase.shape, jnp.float32),
            pltpu.SMEM((2,) + pulse_phase.shape, jnp.float32),
            pltpu.SemaphoreType.DMA,
            pltpu.VMEM((2, 4 * hop_bins, LANES), jnp.bfloat16),
            pltpu.VMEM((pulses, extended, LANES), jnp.float32),
            pltpu.VMEM((beams, extended, LANES), jnp.float32),
            pltpu.VMEM((1, extended, LANES), jnp.float32),
            pltpu.VMEM((2, span, hop_bins + 2 * SHIFT, LANES), jnp.float32),
            pltpu.VMEM((2, 2 * beams, hop_bins, LANES), jnp.float32),
            pltpu.VMEM((levels, span, hop_bins, LANES), jnp.bfloat16),
            pltpu.VMEM((levels, span, hop_bins, LANES), jnp.bfloat16),
            pltpu.VMEM((beams * LANES, hop_bins), jnp.float32),
            pltpu.SemaphoreType.DMA((levels, span)),
            pltpu.SemaphoreType.DMA((levels, span)),
        ],
        compiler_params=pltpu.CompilerParams(
            collective_id=0, has_side_effects=True, vmem_limit_bytes=48 * 2**20
        ),
    )(*[pltpu.with_memory_space_constraint(operand, pltpu.HBM) for operand in operands])


def local_any(raw_echoes, *rest):
    pulses, blocks, parts, hop_bins = raw_echoes.shape
    paired = lax.axis_size("pulse") % 2**LEVELS == 0
    if lax.axis_size("rng") == 1 and blocks * parts == LANES and hop_bins == LANES and paired:
        return local_fused(raw_echoes, *rest)
    return local(raw_echoes, *rest)


def solution(mesh):
    in_specs = (
        P(("grp", "pulse"), "rng", None, None),
        P(),
        P(("grp", "pulse"), None),
        P(("grp", "pulse"), None),
        P(),
        P(),
        P(),
        P(),
        P(),
    )
    out_specs = P(None, ("grp", "pulse"), "rng")
    return jax.shard_map(local_any, mesh=mesh, in_specs=in_specs, out_specs=out_specs, check_vma=False)
```
